32 devices in a mesh: seq: 4 (over x, core), ctx: 8 (over z, y).
Axes of the slice: x: 2, y: 2, z: 4, core: 2. Of those that a mesh axis runs over, the one named last changes fastest.
Arguments:
- tokens: bfloat16 [4096, 2048], P(('seq', 'ctx')), may hold values from -6 to 6
- prefix: int32 [4], P('seq'), may hold values from 102 to 512
- span_order: int32 [4, 16], P('seq'), may hold values from 0 to 15, as said below
- w_query: bfloat16 [2048, 2048], P(('seq', 'ctx')), may hold values from -0.125 to 0.125
- w_key: bfloat16 [1024, 2048], P(('seq', 'ctx')), may hold values from -0.125 to 0.125
- w_value: bfloat16 [1024, 2048], P(('seq', 'ctx')), may hold values from -0.125 to 0.125
- w_out: bfloat16 [2048, 2048], P(('seq', 'ctx')), may hold values from -6 to 6
- w_headgate: bfloat16 [16, 2048], P(None, ('seq', 'ctx')), may hold values from -0.125 to 0.125
- attn_gain: bfloat16 [2048], P(('seq', 'ctx')), may hold values from 0.25 to 1.75
- query_gain: bfloat16 [128], P(('seq', 'ctx')), may hold values from 0.25 to 1.75
- key_gain: bfloat16 [128], P(('seq', 'ctx')), may hold values from 0.25 to 1.75
- mlp_gain: bfloat16 [2048], P(('seq', 'ctx')), may hold values from 0.25 to 1.75
- w_gate: bfloat16 [6144, 2048], P(('seq', 'ctx')), may hold values from -0.125 to 0.125
- w_up: bfloat16 [6144, 2048], P(('seq', 'ctx')), may hold values from -0.125 to 0.125
- w_down: bfloat16 [6144, 2048], P(('seq', 'ctx')), may hold values from -0.078125 to 0.078125
- cotangent: bfloat16 [4096, 2048], P(('seq', 'ctx')), may hold values from -6 to 6
Outputs:
- output: bfloat16 [4096, 2048], P(('seq', 'ctx'))
- grad_tokens: float32 [4096, 2048], P(('seq', 'ctx'))
- grad_w_query: float32 [2048, 2048], P(('seq', 'ctx'))
- grad_w_key: float32 [1024, 2048], P(('seq', 'ctx'))
- grad_w_value: float32 [1024, 2048], P(('seq', 'ctx'))
- grad_w_out: float32 [2048, 2048], P(('seq', 'ctx'))
- grad_w_headgate: float32 [16, 2048], P(None, ('seq', 'ctx'))
- grad_attn_gain: float32 [2048], P(('seq', 'ctx'))
- grad_query_gain: float32 [128], P(('seq', 'ctx'))
- grad_key_gain: float32 [128], P(('seq', 'ctx'))
- grad_mlp_gain: float32 [2048], P(('seq', 'ctx'))
- grad_w_gate: float32 [6144, 2048], P(('seq', 'ctx'))
- grad_w_up: float32 [6144, 2048], P(('seq', 'ctx'))
- grad_w_down: float32 [6144, 2048], P(('seq', 'ctx'))
The draws below stay inside these ranges and needn't reach their ends.
Inputs may be any that keep to these rules, and one draw needn't show every extreme that they name: `span_order`: for every sequence, slots 2c and 2c+1 (the spans of ctx index c) hold a span position p below 8 and its mirror 1024 // 64 - 1 - p; every span position appears exactly once.
All inputs are finite; a program needn't handle non-finite values.
Results may differ from the reference program's by a relative error of at most 0.022.
Values may be sent and summed in bfloat16 or wider, within the bound.
No kernel may reach another device: no remote copies, remote signals or barrier semaphores. Data moves between devices by JAX's collectives and lax.ppermute only.
A program may use at most 320 MiB of HBM per device.

```python
import jax
import jax.numpy as jnp
from jax import lax

D = 2048
H = 16
KVH = 8
HD = 128
FF = 6144
SPAN = 64
LENGTH = 1024
SEQS = 4
TOKENS = 4096


def draw_span_order(key, part):
    count = LENGTH // SPAN
    half = count // 2
    keys = jax.random.split(key, SEQS)

    def one_sequence(seq_key):
        order = jax.random.permutation(seq_key, half).astype(jnp.int32)
        return jnp.stack([order, count - 1 - order], axis=1).reshape(count)
    return jax.vmap(one_sequence)(keys).astype(jnp.int32)


def plant(array, own_key, low, largest):
    place = [jax.random.randint(jax.random.fold_in(own_key, axis), (), 0, length) for axis, length in enumerate(array.shape)]
    main_axis = array.shape.index(max(array.shape))
    neighbour = place[:main_axis] + [(place[main_axis] + 1) % array.shape[main_axis]] + place[main_axis + 1:]
    return array.at[tuple(place)].set(low).at[tuple(neighbour)].set(largest)


def shard_levels(rng, extent, shards, smallest, high):
    loudness = 1.0
    for position, shards_of in shards:
        draws = jax.random.uniform(jax.random.fold_in(jax.random.fold_in(rng, 6), position), (shards_of,), jnp.float32, smallest / len(shards), high / len(shards))
        loudness = loudness * jnp.repeat(jnp.exp(draws), extent[position] // shards_of).reshape((-1,) + (1,) * (len(extent) - 1 - position))
    return loudness


def bell_draw(own_key, shape, deviation, most, shards=(), kind=jnp.bfloat16):
    level = shard_levels(own_key, shape, shards, -0.22, 0.18) if shards else 1.0
    drawn = jax.random.normal(own_key, shape, jnp.float32) * deviation * level
    return jnp.minimum(jnp.maximum(drawn, -most), most).astype(kind)


def setup_inputs(seed: int = 0) -> dict:
    arg_keys = jax.random.split(jax.random.key(seed), 17)
    tokens = bell_draw(arg_keys[0], (TOKENS, D), 1.0, 6.0, ((0, 32),))
    prefix = plant(jax.random.randint(arg_keys[1], (SEQS,), LENGTH // 10, LENGTH // 2 + 1), jax.random.fold_in(arg_keys[1], 1), LENGTH // 10, (LENGTH // 2 + 1) - 1).astype(jnp.int32)
    span_order = draw_span_order(jax.random.fold_in(arg_keys[16], 71), 0)
    w_query = bell_draw(arg_keys[3], (H * HD, D), D ** -0.5, 0.125, ((0, 32),))
    w_key = bell_draw(arg_keys[4], (KVH * HD, D), D ** -0.5, 0.125, ((0, 32),))
    w_value = bell_draw(arg_keys[5], (KVH * HD, D), D ** -0.5, 0.125, ((0, 32),))
    w_out = bell_draw(arg_keys[6], (H * HD, D), 1 ** -0.5, 6.0, ((0, 32),))
    w_headgate = bell_draw(arg_keys[7], (H, D), D ** -0.5, 0.125, ((1, 32),))
    attn_gain = jnp.clip(1.0 + 0.15 * jax.random.normal(arg_keys[8], (D,), jnp.float32), 0.25, 1.75).astype(jnp.bfloat16)
    query_gain = jnp.clip(1.0 + 0.15 * jax.random.normal(arg_keys[9], (HD,), jnp.float32), 0.25, 1.75).astype(jnp.bfloat16)
    key_gain = jnp.clip(1.0 + 0.15 * jax.random.normal(arg_keys[10], (HD,), jnp.float32), 0.25, 1.75).astype(jnp.bfloat16)
    mlp_gain = jnp.clip(1.0 + 0.15 * jax.random.normal(arg_keys[11], (D,), jnp.float32), 0.25, 1.75).astype(jnp.bfloat16)
    w_gate = bell_draw(arg_keys[12], (FF, D), D ** -0.5, 0.125, ((0, 32),))
    w_up = bell_draw(arg_keys[13], (FF, D), D ** -0.5, 0.125, ((0, 32),))
    w_down = bell_draw(arg_keys[14], (FF, D), FF ** -0.5, 0.078125, ((0, 32),))
    cotangent = bell_draw(arg_keys[15], (TOKENS, D), 1.0, 6.0, ((0, 32),))
    return {"tokens": tokens, "prefix": prefix, "span_order": span_order, "w_query": w_query, "w_key": w_key, "w_value": w_value, "w_out": w_out, "w_headgate": w_headgate, "attn_gain": attn_gain, "query_gain": query_gain, "key_gain": key_gain, "mlp_gain": mlp_gain, "w_gate": w_gate, "w_up": w_up, "w_down": w_down, "cotangent": cotangent}


EPS = 1e-06
ROPE_BASE = 1000000.0
NEG = -1e+30
HIGH = lax.Precision.HIGHEST

@jax.custom_vjp
def low(v):
    return lax.optimization_barrier(v.astype(jnp.bfloat16)).astype(jnp.float32)

@jax.custom_vjp
def low_back(v):
    return v

def low_keep(v):
    return (low(v), None)

def low_pass(kept, grad):
    return (grad,)

def back_keep(v):
    return (v, None)

def back_low(kept, grad):
    return (low(grad),)
low.defvjp(low_keep, low_pass)
low_back.defvjp(back_keep, back_low)

def rms_norm(v, gain):
    return v * lax.rsqrt(lax.optimization_barrier(jnp.mean(v * v, axis=-1, keepdims=True)) + EPS) * gain

def rotate(v, positions):
    half = v.shape[-1] // 2
    inv_freq = 1.0 / ROPE_BASE ** (jnp.arange(half, dtype=jnp.float32) * 2.0 / v.shape[-1])
    angles = positions.astype(jnp.float32)[:, None] * inv_freq[None, :]
    cosine = jnp.cos(angles)[:, None, :]
    sine = jnp.sin(angles)[:, None, :]
    first = v[..., :half]
    second = v[..., half:]
    return jnp.concatenate([first * cosine - second * sine, second * cosine + first * sine], axis=-1)

def sequence_forward(x, weights, positions, prefix_len):
    wq, wk, wv, wo, wgt, g1, gq, gk, g2, wg, wu, wd = weights
    xn1 = low(rms_norm(x, g1))
    query = low_back(jnp.dot(xn1, wq.T, precision=HIGH)).reshape(LENGTH, H, HD)
    key = low_back(jnp.dot(xn1, wk.T, precision=HIGH)).reshape(LENGTH, KVH, HD)
    value = low_back(low(jnp.dot(xn1, wv.T, precision=HIGH))).reshape(LENGTH, KVH, HD)
    logits = low_back(jnp.dot(xn1, wgt.T, precision=HIGH))
    query_rot = low_back(low(rotate(rms_norm(query, gq), positions)))
    key_rot = low_back(low(rotate(rms_norm(key, gk), positions)))
    limit = jnp.maximum(positions, prefix_len - 1)
    allowed = positions[None, :] <= limit[:, None]
    q_groups = query_rot.reshape(LENGTH, KVH, H // KVH, HD).transpose(1, 2, 0, 3)
    keys = key_rot.transpose(1, 0, 2)
    values = value.transpose(1, 0, 2)

    def one_head(item):
        qh, kh, vh = item
        scores = low_back(jnp.einsum('gqd,kd->gqk', qh, kh, precision=HIGH) * HD ** (-0.5))
        scores = jnp.where(allowed[None], scores, NEG)
        probs = jnp.exp(scores - jax.nn.logsumexp(scores, axis=-1, keepdims=True))
        return jnp.einsum('gqk,kd->gqd', low(probs), vh, precision=HIGH)
    attended = lax.map(jax.checkpoint(one_head), (q_groups, keys, values))
    attended = low_back(attended.transpose(2, 0, 1, 3).reshape(LENGTH, H, HD))
    gates = jax.nn.sigmoid(logits)
    mixed = low((attended * gates[:, :, None]).reshape(LENGTH, H * HD))
    hidden1 = x + low_back(jnp.dot(mixed, wo, precision=HIGH))
    xn2 = low(rms_norm(hidden1, g2))
    gate = low_back(jnp.dot(xn2, wg.T, precision=HIGH))
    up = low_back(jnp.dot(xn2, wu.T, precision=HIGH))
    act = low(jax.nn.silu(gate) * up)
    return hidden1 + low_back(jnp.dot(act, wd, precision=HIGH))

def reference(tokens, prefix, span_order, w_query, w_key, w_value, w_out, w_headgate, attn_gain, query_gain, key_gain, mlp_gain, w_gate, w_up, w_down, cotangent):
    offsets = jnp.arange(SPAN, dtype=jnp.int32)
    positions = (span_order[:, :, None] * SPAN + offsets[None, None, :]).reshape(SEQS, LENGTH).astype(jnp.int32)
    weights = tuple((w.astype(jnp.float32) for w in (w_query, w_key, w_value, w_out, w_headgate, attn_gain, query_gain, key_gain, mlp_gain, w_gate, w_up, w_down)))
    inputs = tokens.astype(jnp.float32).reshape(SEQS, LENGTH, D)

    def forward(inputs, weights):

        def step(carry, item):
            x, pos, pre = item
            result = jax.checkpoint(lambda a, w: sequence_forward(a, w, pos, pre))(x, weights)
            return (carry, result)
        _, out = lax.scan(step, jnp.zeros((), jnp.float32), (inputs, positions, prefix))
        return out
    out, pullback = jax.vjp(forward, inputs, weights)
    grad_in, grad_w = pullback(cotangent.astype(jnp.float32).reshape(SEQS, LENGTH, D))
    g_wq, g_wk, g_wv, g_wo, g_wgt, g_g1, g_gq, g_gk, g_g2, g_wg, g_wu, g_wd = grad_w
    return (out.reshape(TOKENS, D).astype(jnp.bfloat16), grad_in.reshape(TOKENS, D), g_wq, g_wk, g_wv, g_wo, g_wgt, g_g1, g_gq, g_gk, g_g2, g_wg, g_wu, g_wd)
```

```python
import jax
import jax.numpy as jnp
from jax import lax
from jax.experimental import pallas as pl
from jax.experimental.pallas import tpu as pltpu
from jax.sharding import PartitionSpec as P

H = 16
KVH = 8
HD = 128


EPS = 1e-06
ROPE_BASE = 1000000.0
NEG = -1e30


def rotate(v, positions, sign):
    half = v.shape[-1] // 2
    inv_freq = 1.0 / ROPE_BASE ** (jnp.arange(half, dtype=jnp.float32) * 2.0 / v.shape[-1])
    angles = positions.astype(jnp.float32)[:, None] * inv_freq[None, :]
    cosine = jnp.cos(angles)[:, None, :]
    sine = sign * jnp.sin(angles)[:, None, :]
    first = v[..., :half]
    second = v[..., half:]
    return jnp.concatenate(
        [first * cosine - second * sine, second * cosine + first * sine], axis=-1
    )


def norm_apply(v, gain):
    factor = lax.rsqrt(jnp.mean(v * v, axis=-1, keepdims=True) + EPS)
    return (v * factor * gain, factor)


def norm_back(v, factor, gain, grad):
    weighted = grad * gain
    grad_v = factor * weighted - v * (factor * factor * factor) * jnp.mean(
        weighted * v, axis=-1, keepdims=True
    )
    return (grad_v, grad * v * factor)


def project(left, right):
    return lax.dot_general(
        left, right, (((1,), (1,)), ((), ())), preferred_element_type=jnp.float32
    )


def outer(left, right):
    return lax.dot_general(
        left, right, (((0,), (0,)), ((), ())), preferred_element_type=jnp.float32
    )


def block_scores(query_block, key_block, allowed, factor):
    scores = (
        jnp.einsum("hgtd,khd->hgtk", query_block, key_block, preferred_element_type=jnp.float32)
        * factor
    )
    return jnp.where(allowed[None, None], scores, NEG)


def per_device(
    tokens,
    prefix,
    span_order,
    w_query,
    w_key,
    w_value,
    w_out,
    w_headgate,
    attn_gain,
    query_gain,
    key_gain,
    mlp_gain,
    w_gate,
    w_up,
    w_down,
    cotangent,
):
    rows = tokens.shape[0]
    span = rows // 2
    length = rows * lax.axis_size("ctx")
    heads = H
    kv_heads = KVH
    head = HD
    group = heads // kv_heads
    pair = 2
    pairs = kv_heads // pair
    factor = head ** (-0.5)
    order = span_order[0]
    offsets = jnp.arange(span, dtype=jnp.int32)
    every_pos = (order[:, None] * span + offsets[None, :]).reshape(length)
    mine = lax.dynamic_slice_in_dim(every_pos, lax.axis_index("ctx") * rows, rows)
    limit = jnp.maximum(mine, prefix[0] - 1)
    allowed = every_pos[None, :] <= limit[:, None]
    wq, wk, wv, wo, wgt, g1, gq, gk, g2 = (
        lax.all_gather(w_query, ("seq", "ctx"), axis=0, tiled=True),
        lax.all_gather(w_key, ("seq", "ctx"), axis=0, tiled=True),
        lax.all_gather(w_value, ("seq", "ctx"), axis=0, tiled=True),
        lax.all_gather(w_out, ("seq", "ctx"), axis=0, tiled=True),
        lax.all_gather(w_headgate, ("seq", "ctx"), axis=1, tiled=True),
        lax.all_gather(attn_gain, ("seq", "ctx"), axis=0, tiled=True),
        lax.all_gather(query_gain, ("seq", "ctx"), axis=0, tiled=True),
        lax.all_gather(key_gain, ("seq", "ctx"), axis=0, tiled=True),
        lax.all_gather(mlp_gain, ("seq", "ctx"), axis=0, tiled=True),
    )
    x = tokens.astype(jnp.float32)
    xn1_full, scale1 = norm_apply(x, g1.astype(jnp.float32))
    xn1 = xn1_full.astype(jnp.bfloat16)
    query = project(xn1, wq).reshape(rows, heads, head)
    key = project(xn1, wk).reshape(rows, kv_heads, head)
    value = project(xn1, wv).astype(jnp.bfloat16)
    logits = project(xn1, wgt)
    query_normed, query_scale = norm_apply(query, gq.astype(jnp.float32))
    key_normed, key_scale = norm_apply(key, gk.astype(jnp.float32))
    query_rot = rotate(query_normed, mine, 1.0).astype(jnp.bfloat16)
    key_rot = rotate(key_normed, mine, 1.0).astype(jnp.bfloat16).reshape(rows, kv_heads * head)
    keys_all, values_all = (
        lax.all_gather(key_rot, "ctx", axis=0, tiled=True),
        lax.all_gather(value, "ctx", axis=0, tiled=True),
    )
    query_blocks = query_rot.reshape(rows, pairs, pair, group, head).transpose(1, 2, 3, 0, 4)

    def forward_block(index):
        key_block = lax.dynamic_slice_in_dim(keys_all, index * pair * head, pair * head, 1).reshape(
            length, pair, head
        )
        value_block = lax.dynamic_slice_in_dim(
            values_all, index * pair * head, pair * head, 1
        ).reshape(length, pair, head)
        scores = block_scores(query_blocks[index], key_block, allowed, factor)
        lse = jax.nn.logsumexp(scores, axis=-1, keepdims=True)
        probs = jnp.exp(scores - lse).astype(jnp.bfloat16)
        return (
            jnp.einsum("hgtk,khd->hgtd", probs, value_block, preferred_element_type=jnp.float32),
            lse,
        )

    attended_blocks, lse_blocks = lax.map(forward_block, jnp.arange(pairs))
    attended = attended_blocks.transpose(3, 0, 1, 2, 4).reshape(rows, heads, head)
    gates = jax.nn.sigmoid(logits)
    mixed = (attended * gates[:, :, None]).reshape(rows, heads * head).astype(jnp.bfloat16)
    hidden1 = x + jnp.dot(mixed, wo, preferred_element_type=jnp.float32)
    xn2_full, scale2 = norm_apply(hidden1, g2.astype(jnp.float32))
    xn2 = xn2_full.astype(jnp.bfloat16)
    gate_local, up_local, down_local = (
        lax.all_gather(w_gate, "seq", axis=0, tiled=True),
        lax.all_gather(w_up, "seq", axis=0, tiled=True),
        lax.all_gather(w_down, "seq", axis=0, tiled=True),
    )
    xn2_all, grad_y_all = (
        lax.all_gather(xn2, "ctx", axis=0, tiled=True),
        lax.all_gather(cotangent, "ctx", axis=0, tiled=True),
    )
    gate_part = project(xn2_all, gate_local)
    up_part = project(xn2_all, up_local)
    act_part = (jax.nn.silu(gate_part) * up_part).astype(jnp.bfloat16)
    branch = lax.psum_scatter(
        jnp.dot(act_part, down_local, preferred_element_type=jnp.float32).astype(jnp.bfloat16),
        "ctx",
        scatter_dimension=0,
        tiled=True,
    ).astype(jnp.float32)
    output = (hidden1 + branch).astype(jnp.bfloat16)
    gate_all = project(xn2_all, gate_local)
    up_all = project(xn2_all, up_local)
    sig_all = jax.nn.sigmoid(gate_all)
    silu_all = gate_all * sig_all
    act_local = (silu_all * up_all).astype(jnp.bfloat16)
    grad_act_all = project(grad_y_all, down_local)
    grad_gate_local = (grad_act_all * up_all * sig_all * (1.0 + gate_all * (1.0 - sig_all))).astype(
        jnp.bfloat16
    )
    grad_up_local = (grad_act_all * silu_all).astype(jnp.bfloat16)
    grad_xn2 = lax.psum_scatter(
        (
            jnp.dot(grad_gate_local, gate_local, preferred_element_type=jnp.float32)
            + jnp.dot(grad_up_local, up_local, preferred_element_type=jnp.float32)
        ).astype(jnp.bfloat16),
        "ctx",
        scatter_dimension=0,
        tiled=True,
    ).astype(jnp.float32)
    grad_w_gate, grad_w_up, grad_w_down = (
        lax.psum_scatter(
            outer(grad_gate_local, xn2_all).astype(jnp.bfloat16),
            "seq",
            scatter_dimension=0,
            tiled=True,
        ).astype(jnp.float32),
        lax.psum_scatter(
            outer(grad_up_local, xn2_all).astype(jnp.bfloat16),
            "seq",
            scatter_dimension=0,
            tiled=True,
        ).astype(jnp.float32),
        lax.psum_scatter(
            outer(act_local, grad_y_all).astype(jnp.bfloat16),
            "seq",
            scatter_dimension=0,
            tiled=True,
        ).astype(jnp.float32),
    )
    grad_h1_norm, gain2_terms = norm_back(hidden1, scale2, g2.astype(jnp.float32), grad_xn2)
    grad_hidden1 = cotangent.astype(jnp.float32) + grad_h1_norm
    grad_gain2 = jnp.sum(gain2_terms, axis=0)
    grad_branch = grad_hidden1.astype(jnp.bfloat16)
    grad_w_out = outer(mixed, grad_branch)
    grad_mixed = project(grad_branch, wo).reshape(rows, heads, head)
    grad_att = (grad_mixed * gates[:, :, None]).astype(jnp.bfloat16)
    grad_logits = (jnp.sum(grad_mixed * attended, axis=-1) * gates * (1.0 - gates)).astype(
        jnp.bfloat16
    )
    grad_blocks = grad_att.reshape(rows, pairs, pair, group, head).transpose(1, 2, 3, 0, 4)

    def backward_block(index):
        key_block = lax.dynamic_slice_in_dim(keys_all, index * pair * head, pair * head, 1).reshape(
            length, pair, head
        )
        value_block = lax.dynamic_slice_in_dim(
            values_all, index * pair * head, pair * head, 1
        ).reshape(length, pair, head)
        query_block = query_blocks[index]
        grad_out = grad_blocks[index]
        scores = block_scores(query_block, key_block, allowed, factor)
        probs = jnp.exp(scores - lse_blocks[index])
        grad_probs = jnp.einsum(
            "hgtd,khd->hgtk", grad_out, value_block, preferred_element_type=jnp.float32
        )
        delta = jnp.sum(probs * grad_probs, axis=-1, keepdims=True)
        grad_scores = (probs * (grad_probs - delta)).astype(jnp.bfloat16)
        grad_query = (
            jnp.einsum("hgtk,khd->hgtd", grad_scores, key_block, preferred_element_type=jnp.float32)
            * factor
        )
        grad_key = (
            jnp.einsum(
                "hgtk,hgtd->khd", grad_scores, query_block, preferred_element_type=jnp.float32
            )
            * factor
        )
        grad_value = jnp.einsum(
            "hgtk,hgtd->khd",
            probs.astype(jnp.bfloat16),
            grad_out,
            preferred_element_type=jnp.float32,
        )
        return (grad_query, grad_key, grad_value)

    grad_query_blocks, grad_key_all, grad_value_all = lax.map(backward_block, jnp.arange(pairs))
    grad_key_sum, grad_value_sum = (
        lax.psum_scatter(
            grad_key_all.astype(jnp.bfloat16), "ctx", scatter_dimension=1, tiled=True
        ).astype(jnp.float32),
        lax.psum_scatter(
            grad_value_all.astype(jnp.bfloat16), "ctx", scatter_dimension=1, tiled=True
        ).astype(jnp.float32),
    )
    grad_value_rows = (
        grad_value_sum.astype(jnp.bfloat16).transpose(1, 0, 2, 3).reshape(rows, kv_heads * head)
    )
    grad_key_rot = (
        grad_key_sum.astype(jnp.bfloat16)
        .astype(jnp.float32)
        .transpose(1, 0, 2, 3)
        .reshape(rows, kv_heads, head)
    )
    grad_key_normed = rotate(grad_key_rot, mine, -1.0)
    grad_key_pre, key_gain_terms = norm_back(
        key, key_scale, gk.astype(jnp.float32), grad_key_normed
    )
    grad_key_rows = grad_key_pre.astype(jnp.bfloat16).reshape(rows, kv_heads * head)
    grad_key_gain = jnp.sum(key_gain_terms, axis=(0, 1))
    grad_query_rot = (
        grad_query_blocks.transpose(3, 0, 1, 2, 4)
        .reshape(rows, heads, head)
        .astype(jnp.bfloat16)
        .astype(jnp.float32)
    )
    grad_query_normed = rotate(grad_query_rot, mine, -1.0)
    grad_query_pre, query_gain_terms = norm_back(
        query, query_scale, gq.astype(jnp.float32), grad_query_normed
    )
    grad_query_rows = grad_query_pre.astype(jnp.bfloat16).reshape(rows, heads * head)
    grad_query_gain = jnp.sum(query_gain_terms, axis=(0, 1))
    grad_w_query = outer(grad_query_rows, xn1)
    grad_w_key = outer(grad_key_rows, xn1)
    grad_w_value = outer(grad_value_rows, xn1)
    grad_w_headgate = outer(grad_logits, xn1)
    grad_xn1 = jnp.dot(grad_query_rows, wq, preferred_element_type=jnp.float32) + jnp.dot(
        grad_key_rows, wk, preferred_element_type=jnp.float32
    )
    grad_xn1 = (
        grad_xn1
        + jnp.dot(grad_value_rows, wv, preferred_element_type=jnp.float32)
        + jnp.dot(grad_logits, wgt, preferred_element_type=jnp.float32)
    )
    grad_x_norm, gain1_terms = norm_back(x, scale1, g1.astype(jnp.float32), grad_xn1)
    grad_tokens = grad_hidden1 + grad_x_norm
    grad_gain1 = jnp.sum(gain1_terms, axis=0)
    summed = (
        lax.psum_scatter(grad_w_query, ("seq", "ctx"), scatter_dimension=0, tiled=True),
        lax.psum_scatter(grad_w_key, ("seq", "ctx"), scatter_dimension=0, tiled=True),
        lax.psum_scatter(grad_w_value, ("seq", "ctx"), scatter_dimension=0, tiled=True),
        lax.psum_scatter(grad_w_out, ("seq", "ctx"), scatter_dimension=0, tiled=True),
        lax.psum_scatter(grad_w_headgate, ("seq", "ctx"), scatter_dimension=1, tiled=True),
        lax.psum_scatter(grad_gain1, ("seq", "ctx"), scatter_dimension=0, tiled=True),
        lax.psum_scatter(grad_query_gain, ("seq", "ctx"), scatter_dimension=0, tiled=True),
        lax.psum_scatter(grad_key_gain, ("seq", "ctx"), scatter_dimension=0, tiled=True),
        lax.psum_scatter(grad_gain2, ("seq", "ctx"), scatter_dimension=0, tiled=True),
    )
    g_wq, g_wk, g_wv, g_wo, g_wgt, g_g1, g_gq, g_gk, g_g2 = summed
    return (
        output,
        grad_tokens,
        g_wq,
        g_wk,
        g_wv,
        g_wo,
        g_wgt,
        g_g1,
        g_gq,
        g_gk,
        g_g2,
        grad_w_gate,
        grad_w_up,
        grad_w_down,
    )


BF16 = jnp.bfloat16
F32 = jnp.float32
BOTH = ("seq", "ctx")


def swap(v, d):
    return lax.ppermute(v, "ctx", [(c, c ^ d) for c in range(8)])


def hop(v, d):
    return lax.ppermute(v, BOTH, [(i, i ^ d) for i in range(32)])


def turn(v):
    pairs = [(8 * r + 4 * q + j, 8 * j + 4 * q + r) for r in range(4) for q in range(2) for j in range(4)]
    return lax.ppermute(v, BOTH, pairs)


def gather_ctx(v, parts=2):
    step = v.shape[0] // parts
    done = []
    for i in range(parts):
        own = v[i * step : (i + 1) * step]
        z1 = swap(own, 2)
        y0 = swap(own, 1)
        z3 = swap(own, 6)
        z2 = swap(own, 4)
        done.append((own, y0, z1, swap(z1, 1), z2, swap(z2, 1), z3, swap(z3, 1)))
    return [[done[i][d] for i in range(parts)] for d in range(8)]


def joined(blocks):
    return jnp.concatenate([p for block in blocks for p in block], axis=0)


def scatter_ctx(blocks):
    kept = {}
    for dz in (3, 2, 1, 0):
        kept[dz] = blocks[2 * dz].astype(F32) + swap(blocks[2 * dz + 1], 1).astype(F32)
    far3 = swap(kept[3].astype(BF16), 4)
    far2 = swap(kept[2].astype(BF16), 4)
    near = (kept[1] + far3.astype(F32)).astype(BF16)
    return kept[0] + far2.astype(F32) + swap(near, 2).astype(F32)


def gather_small(v, flat):
    blocks = v[None]
    for b in range(5):
        other = hop(blocks, 1 << b)
        high = ((flat >> b) & 1) == 1
        blocks = jnp.where(
            high, jnp.concatenate([other, blocks], 0), jnp.concatenate([blocks, other], 0)
        )
    return blocks


def scatter_small(blocks, flat):
    for b in (4, 3, 2, 1, 0):
        half = blocks.shape[0] // 2
        high = ((flat >> b) & 1) == 1
        lower, upper = blocks[:half], blocks[half:]
        blocks = jnp.where(high, upper, lower) + hop(jnp.where(high, lower, upper), 1 << b)
    return blocks[0]


def by_bits(stack, c):
    shape = stack.shape
    stack = stack.reshape((2, 2, 2) + shape[1:])
    for axis, bit in ((0, 4), (1, 2), (2, 1)):
        stack = jnp.where((c & bit) != 0, jnp.flip(stack, axis), stack)
    return stack.reshape(shape)


def attention_kernel(limit_ref, pos_ref, q_ref, k_ref, v_ref, out_ref, lse_ref):
    scores = lax.dot_general(
        q_ref[...], k_ref[...], (((1,), (1,)), ((), ())), preferred_element_type=F32
    ) * (HD**-0.5)
    scores = jnp.where(pos_ref[...] <= limit_ref[...], scores, NEG)
    top = jnp.max(scores, axis=-1, keepdims=True)
    weights = jnp.exp(scores - top)
    total = jnp.sum(weights, axis=-1, keepdims=True)
    probs = (weights * (1.0 / total)).astype(BF16)
    out_ref[...] = jnp.dot(probs, v_ref[...], preferred_element_type=F32)
    lse_ref[0] = top + jnp.log(total)


def attention(q, k, v, limit, pos, tile=256):
    length = q.shape[0]
    group = q.shape[1] // HD
    return pl.pallas_call(
        attention_kernel,
        grid=(group, length // tile),
        in_specs=[
            pl.BlockSpec((tile, 1), lambda h, i: (i, 0)),
            pl.BlockSpec((1, length), lambda h, i: (0, 0)),
            pl.BlockSpec((tile, HD), lambda h, i: (i, h)),
            pl.BlockSpec((length, HD), lambda h, i: (0, 0)),
            pl.BlockSpec((length, HD), lambda h, i: (0, 0)),
        ],
        out_specs=[
            pl.BlockSpec((tile, HD), lambda h, i: (i, h)),
            pl.BlockSpec((1, tile, 1), lambda h, i: (h, i, 0)),
        ],
        out_shape=[
            jax.ShapeDtypeStruct((length, group * HD), F32),
            jax.ShapeDtypeStruct((group, length, 1), F32),
        ],
        cost_estimate=pl.CostEstimate(
            flops=4 * group * length * length * HD,
            bytes_accessed=4 * length * HD * 4,
            transcendentals=group * length * length,
        ),
    )(limit, pos, q, k, v)


def attention_back_kernel(
    limit_ref, pos_ref, q_ref, k_ref, v_ref, lse_ref, g_ref, gq_ref, gk_ref, gv_ref
):
    @pl.when((pl.program_id(0) == 0) & (pl.program_id(1) == 0))
    def _():
        gk_ref[...] = jnp.zeros_like(gk_ref)
        gv_ref[...] = jnp.zeros_like(gv_ref)

    scores = lax.dot_general(
        q_ref[...], k_ref[...], (((1,), (1,)), ((), ())), preferred_element_type=F32
    ) * (HD**-0.5)
    scores = jnp.where(pos_ref[...] <= limit_ref[...], scores, NEG)
    probs = jnp.exp(scores - lse_ref[0])
    grad_probs = lax.dot_general(
        g_ref[...], v_ref[...], (((1,), (1,)), ((), ())), preferred_element_type=F32
    )
    delta = jnp.sum(probs * grad_probs, axis=-1, keepdims=True)
    grad_scores = (probs * (grad_probs - delta)).astype(BF16)
    gq_ref[...] = jnp.dot(grad_scores, k_ref[...], preferred_element_type=F32) * (HD**-0.5)
    gk_ref[...] += lax.dot_general(
        grad_scores, q_ref[...], (((0,), (0,)), ((), ())), preferred_element_type=F32
    ) * (HD**-0.5)
    gv_ref[...] += lax.dot_general(
        probs.astype(BF16), g_ref[...], (((0,), (0,)), ((), ())), preferred_element_type=F32
    )


def attention_back(q, k, v, lse, grad, limit, pos, tile=256):
    length = q.shape[0]
    group = q.shape[1] // HD
    return pl.pallas_call(
        attention_back_kernel,
        grid=(group, length // tile),
        in_specs=[
            pl.BlockSpec((tile, 1), lambda h, i: (i, 0)),
            pl.BlockSpec((1, length), lambda h, i: (0, 0)),
            pl.BlockSpec((tile, HD), lambda h, i: (i, h)),
            pl.BlockSpec((length, HD), lambda h, i: (0, 0)),
            pl.BlockSpec((length, HD), lambda h, i: (0, 0)),
            pl.BlockSpec((1, tile, 1), lambda h, i: (h, i, 0)),
            pl.BlockSpec((tile, HD), lambda h, i: (i, h)),
        ],
        out_specs=[
            pl.BlockSpec((tile, HD), lambda h, i: (i, h)),
            pl.BlockSpec((length, HD), lambda h, i: (0, 0)),
            pl.BlockSpec((length, HD), lambda h, i: (0, 0)),
        ],
        out_shape=[
            jax.ShapeDtypeStruct((length, group * HD), F32),
            jax.ShapeDtypeStruct((length, HD), F32),
            jax.ShapeDtypeStruct((length, HD), F32),
        ],
        cost_estimate=pl.CostEstimate(
            flops=10 * group * length * length * HD,
            bytes_accessed=8 * length * HD * 4,
            transcendentals=group * length * length,
        ),
    )(limit, pos, q, k, v, lse, grad)


def turned(v, cosine, sine):
    first = v[..., : HD // 2]
    second = v[..., HD // 2 :]
    return jnp.concatenate(
        [first * cosine - second * sine, second * cosine + first * sine], axis=-1
    )


def per_device_small(
    tokens,
    prefix,
    span_order,
    w_query,
    w_key,
    w_value,
    w_out,
    w_headgate,
    attn_gain,
    query_gain,
    key_gain,
    mlp_gain,
    w_gate,
    w_up,
    w_down,
    cotangent,
):
    rows, width = tokens.shape
    length = 8 * rows
    span = rows // 2
    group = H // KVH
    s = lax.axis_index("seq")
    c = lax.axis_index("ctx")
    flat = 8 * s + c
    mine = 2 * (c & 3) + (c >> 2)

    small = jnp.concatenate(
        [
            w_headgate,
            attn_gain[None],
            mlp_gain[None],
            jnp.pad(jnp.concatenate([query_gain, key_gain]), (0, 56))[None],
            jnp.zeros((13, 64), BF16),
        ],
        axis=0,
    )
    smalls = gather_small(small, flat)
    wgt = smalls[:, :16].transpose(1, 0, 2).reshape(H, width)
    g1 = smalls[:, 16].reshape(width).astype(F32)
    g2 = smalls[:, 17].reshape(width).astype(F32)
    gq = smalls[:, 18, :4].reshape(HD).astype(F32)
    gk = smalls[:, 18, 4:8].reshape(HD).astype(F32)

    packed = turn(jnp.concatenate([w_query, w_key, w_value], axis=0))
    packed = lax.all_gather(packed, "seq", axis=0)
    w_qkv = jnp.concatenate(
        [
            packed[:, :64].reshape(256, width),
            packed[:, 64:96].reshape(128, width),
            packed[:, 96:].reshape(128, width),
        ],
        axis=0,
    )
    wo = lax.all_gather(w_out, BOTH, axis=0, tiled=True)
    wg = lax.all_gather(w_gate, "seq", axis=0, tiled=True)
    wu = lax.all_gather(w_up, "seq", axis=0, tiled=True)
    wd = lax.all_gather(w_down, "seq", axis=0, tiled=True)

    order = span_order[0].reshape(8, 2)
    order = by_bits(order, c)
    pos = (order[:, :, None] * span + jnp.arange(span, dtype=jnp.int32)).reshape(length)
    limit = jnp.maximum(pos, prefix[0] - 1)
    half = HD // 2
    inv_freq = 1.0 / ROPE_BASE ** (jnp.arange(half, dtype=F32) * 2.0 / HD)
    angles = pos.astype(F32)[:, None] * inv_freq[None, :]
    cosine, sine = lax.optimization_barrier((jnp.cos(angles), jnp.sin(angles)))
    limit = limit[:, None]
    pos = pos[None, :]

    x_all = joined(gather_ctx(tokens))
    cot_all = joined(gather_ctx(cotangent))

    xf = x_all.astype(F32)
    scale1 = lax.rsqrt(jnp.mean(xf * xf, axis=-1, keepdims=True) + EPS)
    xn1 = (xf * scale1 * g1).astype(BF16)
    qkv = project(xn1, w_qkv)
    wgt2 = lax.dynamic_slice_in_dim(wgt, 2 * mine, 2, 0)
    gates = jax.nn.sigmoid(project(xn1, wgt2))
    query = qkv[:, : group * HD].reshape(length, group, HD)
    key = qkv[:, group * HD : (group + 1) * HD]
    value = qkv[:, (group + 1) * HD :].astype(BF16)
    query_normed, query_scale = norm_apply(query, gq)
    key_normed, key_scale = norm_apply(key, gk)
    query_rot = (
        turned(query_normed, cosine[:, None], sine[:, None]).astype(BF16).reshape(length, group * HD)
    )
    key_rot = turned(key_normed, cosine, sine).astype(BF16)
    attended, lse = attention(query_rot, key_rot, value, limit, pos)
    spread = jnp.repeat(gates, HD, axis=1)
    mixed = (attended * spread).astype(BF16)

    got = [mixed[:rows]] + [swap(mixed[d * rows : (d + 1) * rows], d) for d in range(1, 8)]
    stack = by_bits(jnp.stack(got), c).reshape(2, 4, rows, group * HD)
    mixed_own = stack.transpose(2, 1, 0, 3).reshape(rows, width)
    x = tokens.astype(F32)
    hidden1 = x + jnp.dot(mixed_own, wo, preferred_element_type=F32)
    xn2_full, scale2 = norm_apply(hidden1, g2)
    xn2_all = joined(gather_ctx(xn2_full.astype(BF16)))

    gate = project(xn2_all, wg)
    up = project(xn2_all, wu)
    grad_act = project(cot_all, wd)
    sig = jax.nn.sigmoid(gate)
    silu = gate * sig
    act = (silu * up).astype(BF16)
    grad_gate = (grad_act * up * sig * (1.0 + gate * (1.0 - sig))).astype(BF16)
    grad_up = (grad_act * silu).astype(BF16)
    grad_xn2_part = (
        jnp.dot(grad_gate, wg, preferred_element_type=F32)
        + jnp.dot(grad_up, wu, preferred_element_type=F32)
    ).astype(BF16)
    grad_xn2 = scatter_ctx([grad_xn2_part[d * rows : (d + 1) * rows] for d in range(8)])
    branch_part = jnp.dot(act, wd, preferred_element_type=F32).astype(BF16)
    branch = scatter_ctx([branch_part[d * rows : (d + 1) * rows] for d in range(8)])
    output = (hidden1 + branch).astype(BF16)
    grad_w_gate, grad_w_up, grad_w_down = (
        lax.psum_scatter(
            outer(left, right).astype(BF16), "seq", scatter_dimension=0, tiled=True
        ).astype(F32)
        for left, right in ((grad_gate, xn2_all), (grad_up, xn2_all), (act, cot_all))
    )

    grad_h1_norm, gain2_terms = norm_back(hidden1, scale2, g2, grad_xn2)
    grad_hidden1 = cotangent.astype(F32) + grad_h1_norm
    grad_gain2 = jnp.sum(gain2_terms, axis=0)
    grad_branch = grad_hidden1.astype(BF16)
    grad_mixed_own = project(grad_branch, wo).astype(BF16)
    stack = by_bits(
        grad_mixed_own.reshape(rows, 4, 2, group * HD).transpose(2, 1, 0, 3).reshape(8, rows, group * HD), c
    )
    grad_mixed = jnp.concatenate(
        [stack[0]] + [swap(stack[d], d) for d in range(1, 8)], axis=0
    ).astype(F32)
    grad_branch_all = joined(gather_ctx(grad_branch))
    grad_wo_part = outer(mixed, grad_branch_all)

    grad_att = (grad_mixed * spread).astype(BF16)
    grad_logits = (
        jnp.sum((grad_mixed * attended).reshape(length, group, HD), axis=-1) * gates * (1.0 - gates)
    ).astype(BF16)
    gq_rot, gk_rot, gv_rows = attention_back(
        query_rot, key_rot, value, lse, grad_att, limit, pos
    )
    gv_rows = gv_rows.astype(BF16)
    gk_normed = turned(gk_rot.astype(BF16).astype(F32), cosine, -sine)
    gk_pre, key_gain_terms = norm_back(key, key_scale, gk, gk_normed)
    gq_normed = turned(
        gq_rot.astype(BF16).astype(F32).reshape(length, group, HD), cosine[:, None], -sine[:, None]
    )
    gq_pre, query_gain_terms = norm_back(query, query_scale, gq, gq_normed)
    grad_gk = jnp.sum(key_gain_terms, axis=0)
    grad_gq = jnp.sum(query_gain_terms, axis=(0, 1))
    grad_qkv = jnp.concatenate(
        [gq_pre.astype(BF16).reshape(length, group * HD), gk_pre.astype(BF16), gv_rows], axis=1
    )
    gl = grad_logits.astype(F32)
    wgt2f = wgt2.astype(F32)
    grad_xn1_part = (
        jnp.dot(grad_qkv, w_qkv, preferred_element_type=F32)
        + gl[:, 0:1] * wgt2f[0:1]
        + gl[:, 1:2] * wgt2f[1:2]
    )
    grad_gain1 = jnp.sum(grad_xn1_part * (xf * scale1), axis=0)
    grad_xn1_part = grad_xn1_part.astype(BF16)
    grad_xn1 = scatter_ctx([grad_xn1_part[d * rows : (d + 1) * rows] for d in range(8)])
    scale1_own = scale1[:rows]
    weighted = grad_xn1 * g1
    grad_tokens = grad_hidden1 + (
        scale1_own * weighted
        - x * (scale1_own * scale1_own * scale1_own) * jnp.mean(weighted * x, axis=-1, keepdims=True)
    )

    grad_w_qkv = outer(grad_qkv, xn1).astype(BF16)
    grad_wo_part = grad_wo_part.astype(BF16)
    pieces = jnp.concatenate(
        [
            grad_w_qkv[:256].reshape(4, 64, width),
            grad_w_qkv[256:384].reshape(4, 32, width),
            grad_w_qkv[384:].reshape(4, 32, width),
            grad_wo_part.reshape(4, 64, width),
        ],
        axis=1,
    ).reshape(4 * 192, width)
    home = turn(lax.psum_scatter(pieces, "seq", scatter_dimension=0, tiled=True)).astype(F32)
    g_wq, g_wk, g_wv, g_wo = home[:64], home[64:96], home[96:128], home[128:]

    grad_wgt = lax.dot_general(
        grad_logits, xn1, (((0,), (0,)), ((), ())), preferred_element_type=F32
    )
    grad_wgt = lax.dynamic_update_slice_in_dim(jnp.zeros((H, width), F32), grad_wgt, 2 * mine, 0)
    bundle = jnp.concatenate(
        [
            grad_wgt.reshape(H, 32, 64).transpose(1, 0, 2),
            grad_gain1.reshape(32, 1, 64),
            grad_gain2.reshape(32, 1, 64),
            jnp.concatenate(
                [grad_gq.reshape(32, 1, 4), grad_gk.reshape(32, 1, 4), jnp.zeros((32, 1, 56), F32)], axis=2
            ),
            jnp.zeros((32, 5, 64), F32),
        ],
        axis=1,
    )
    bundle = scatter_small(bundle, flat)
    return (
        output,
        grad_tokens,
        g_wq,
        g_wk,
        g_wv,
        g_wo,
        bundle[:16],
        bundle[16],
        bundle[18, :4],
        bundle[18, 4:8],
        bundle[17],
        grad_w_gate,
        grad_w_up,
        grad_w_down,
    )


def solution(mesh):
    in_specs = (
        P(("seq", "ctx"), None),
        P("seq"),
        P("seq", None),
        P(("seq", "ctx"), None),
        P(("seq", "ctx"), None),
        P(("seq", "ctx"), None),
        P(("seq", "ctx"), None),
        P(None, ("seq", "ctx")),
        P(("seq", "ctx")),
        P(("seq", "ctx")),
        P(("seq", "ctx")),
        P(("seq", "ctx")),
        P(("seq", "ctx"), None),
        P(("seq", "ctx"), None),
        P(("seq", "ctx"), None),
        P(("seq", "ctx"), None),
    )
    out_specs = (
        P(("seq", "ctx"), None),
        P(("seq", "ctx"), None),
        P(("seq", "ctx"), None),
        P(("seq", "ctx"), None),
        P(("seq", "ctx"), None),
        P(("seq", "ctx"), None),
        P(None, ("seq", "ctx")),
        P(("seq", "ctx")),
        P(("seq", "ctx")),
        P(("seq", "ctx")),
        P(("seq", "ctx")),
        P(("seq", "ctx"), None),
        P(("seq", "ctx"), None),
        P(("seq", "ctx"), None),
    )
    sizes = dict(mesh.shape)
    small = sizes == {"seq": 4, "ctx": 8}
    return jax.shard_map(
        per_device_small if small else per_device, mesh=mesh, in_specs=in_specs, out_specs=out_specs, check_vma=False
    )
```

```python
import jax
import jax.numpy as jnp
from jax import lax
from jax.experimental import pallas as pl
from jax.experimental.pallas import tpu as pltpu

from jax.sharding import PartitionSpec as P

H = 16
KVH = 8
HD = 128


EPS = 1e-06
ROPE_BASE = 1000000.0
NEG = -1e30


def rotate(v, positions, sign):
    half = v.shape[-1] // 2
    inv_freq = 1.0 / ROPE_BASE ** (jnp.arange(half, dtype=jnp.float32) * 2.0 / v.shape[-1])
    angles = positions.astype(jnp.float32)[:, None] * inv_freq[None, :]
    cosine = jnp.cos(angles)[:, None, :]
    sine = sign * jnp.sin(angles)[:, None, :]
    first = v[..., :half]
    second = v[..., half:]
    return jnp.concatenate(
        [first * cosine - second * sine, second * cosine + first * sine], axis=-1
    )


def norm_apply(v, gain):
    factor = lax.rsqrt(jnp.mean(v * v, axis=-1, keepdims=True) + EPS)
    return (v * factor * gain, factor)


def norm_back(v, factor, gain, grad):
    weighted = grad * gain
    grad_v = factor * weighted - v * (factor * factor * factor) * jnp.mean(
        weighted * v, axis=-1, keepdims=True
    )
    return (grad_v, grad * v * factor)


def project(left, right):
    return lax.dot_general(
        left, right, (((1,), (1,)), ((), ())), preferred_element_type=jnp.float32
    )


def outer(left, right):
    return lax.dot_general(
        left, right, (((0,), (0,)), ((), ())), preferred_element_type=jnp.float32
    )


def block_scores(query_block, key_block, allowed, factor):
    scores = (
        jnp.einsum("hgtd,khd->hgtk", query_block, key_block, preferred_element_type=jnp.float32)
        * factor
    )
    return jnp.where(allowed[None, None], scores, NEG)


def per_device(
    tokens,
    prefix,
    span_order,
    w_query,
    w_key,
    w_value,
    w_out,
    w_headgate,
    attn_gain,
    query_gain,
    key_gain,
    mlp_gain,
    w_gate,
    w_up,
    w_down,
    cotangent,
):
    rows = tokens.shape[0]
    span = rows // 2
    length = rows * lax.axis_size("ctx")
    heads = H
    kv_heads = KVH
    head = HD
    group = heads // kv_heads
    pair = 2
    pairs = kv_heads // pair
    factor = head ** (-0.5)
    order = span_order[0]
    offsets = jnp.arange(span, dtype=jnp.int32)
    every_pos = (order[:, None] * span + offsets[None, :]).reshape(length)
    mine = lax.dynamic_slice_in_dim(every_pos, lax.axis_index("ctx") * rows, rows)
    limit = jnp.maximum(mine, prefix[0] - 1)
    allowed = every_pos[None, :] <= limit[:, None]
    wq, wk, wv, wo, wgt, g1, gq, gk, g2 = (
        lax.all_gather(w_query, ("seq", "ctx"), axis=0, tiled=True),
        lax.all_gather(w_key, ("seq", "ctx"), axis=0, tiled=True),
        lax.all_gather(w_value, ("seq", "ctx"), axis=0, tiled=True),
        lax.all_gather(w_out, ("seq", "ctx"), axis=0, tiled=True),
        lax.all_gather(w_headgate, ("seq", "ctx"), axis=1, tiled=True),
        lax.all_gather(attn_gain, ("seq", "ctx"), axis=0, tiled=True),
        lax.all_gather(query_gain, ("seq", "ctx"), axis=0, tiled=True),
        lax.all_gather(key_gain, ("seq", "ctx"), axis=0, tiled=True),
        lax.all_gather(mlp_gain, ("seq", "ctx"), axis=0, tiled=True),
    )
    x = tokens.astype(jnp.float32)
    xn1_full, scale1 = norm_apply(x, g1.astype(jnp.float32))
    xn1 = xn1_full.astype(jnp.bfloat16)
    query = project(xn1, wq).reshape(rows, heads, head)
    key = project(xn1, wk).reshape(rows, kv_heads, head)
    value = project(xn1, wv).astype(jnp.bfloat16)
    logits = project(xn1, wgt)
    query_normed, query_scale = norm_apply(query, gq.astype(jnp.float32))
    key_normed, key_scale = norm_apply(key, gk.astype(jnp.float32))
    query_rot = rotate(query_normed, mine, 1.0).astype(jnp.bfloat16)
    key_rot = rotate(key_normed, mine, 1.0).astype(jnp.bfloat16).reshape(rows, kv_heads * head)
    keys_all, values_all = (
        lax.all_gather(key_rot, "ctx", axis=0, tiled=True),
        lax.all_gather(value, "ctx", axis=0, tiled=True),
    )
    query_blocks = query_rot.reshape(rows, pairs, pair, group, head).transpose(1, 2, 3, 0, 4)

    def forward_block(index):
        key_block = lax.dynamic_slice_in_dim(keys_all, index * pair * head, pair * head, 1).reshape(
            length, pair, head
        )
        value_block = lax.dynamic_slice_in_dim(
            values_all, index * pair * head, pair * head, 1
        ).reshape(length, pair, head)
        scores = block_scores(query_blocks[index], key_block, allowed, factor)
        lse = jax.nn.logsumexp(scores, axis=-1, keepdims=True)
        probs = jnp.exp(scores - lse).astype(jnp.bfloat16)
        return (
            jnp.einsum("hgtk,khd->hgtd", probs, value_block, preferred_element_type=jnp.float32),
            lse,
        )

    attended_blocks, lse_blocks = lax.map(forward_block, jnp.arange(pairs))
    attended = attended_blocks.transpose(3, 0, 1, 2, 4).reshape(rows, heads, head)
    gates = jax.nn.sigmoid(logits)
    mixed = (attended * gates[:, :, None]).reshape(rows, heads * head).astype(jnp.bfloat16)
    hidden1 = x + jnp.dot(mixed, wo, preferred_element_type=jnp.float32)
    xn2_full, scale2 = norm_apply(hidden1, g2.astype(jnp.float32))
    xn2 = xn2_full.astype(jnp.bfloat16)
    gate_local, up_local, down_local = (
        lax.all_gather(w_gate, "seq", axis=0, tiled=True),
        lax.all_gather(w_up, "seq", axis=0, tiled=True),
        lax.all_gather(w_down, "seq", axis=0, tiled=True),
    )
    xn2_all, grad_y_all = (
        lax.all_gather(xn2, "ctx", axis=0, tiled=True),
        lax.all_gather(cotangent, "ctx", axis=0, tiled=True),
    )
    gate_part = project(xn2_all, gate_local)
    up_part = project(xn2_all, up_local)
    act_part = (jax.nn.silu(gate_part) * up_part).astype(jnp.bfloat16)
    branch = lax.psum_scatter(
        jnp.dot(act_part, down_local, preferred_element_type=jnp.float32).astype(jnp.bfloat16),
        "ctx",
        scatter_dimension=0,
        tiled=True,
    ).astype(jnp.float32)
    output = (hidden1 + branch).astype(jnp.bfloat16)
    gate_all = project(xn2_all, gate_local)
    up_all = project(xn2_all, up_local)
    sig_all = jax.nn.sigmoid(gate_all)
    silu_all = gate_all * sig_all
    act_local = (silu_all * up_all).astype(jnp.bfloat16)
    grad_act_all = project(grad_y_all, down_local)
    grad_gate_local = (grad_act_all * up_all * sig_all * (1.0 + gate_all * (1.0 - sig_all))).astype(
        jnp.bfloat16
    )
    grad_up_local = (grad_act_all * silu_all).astype(jnp.bfloat16)
    grad_xn2 = lax.psum_scatter(
        (
            jnp.dot(grad_gate_local, gate_local, preferred_element_type=jnp.float32)
            + jnp.dot(grad_up_local, up_local, preferred_element_type=jnp.float32)
        ).astype(jnp.bfloat16),
        "ctx",
        scatter_dimension=0,
        tiled=True,
    ).astype(jnp.float32)
    grad_w_gate, grad_w_up, grad_w_down = (
        lax.psum_scatter(
            outer(grad_gate_local, xn2_all).astype(jnp.bfloat16),
            "seq",
            scatter_dimension=0,
            tiled=True,
        ).astype(jnp.float32),
        lax.psum_scatter(
            outer(grad_up_local, xn2_all).astype(jnp.bfloat16),
            "seq",
            scatter_dimension=0,
            tiled=True,
        ).astype(jnp.float32),
        lax.psum_scatter(
            outer(act_local, grad_y_all).astype(jnp.bfloat16),
            "seq",
            scatter_dimension=0,
            tiled=True,
        ).astype(jnp.float32),
    )
    grad_h1_norm, gain2_terms = norm_back(hidden1, scale2, g2.astype(jnp.float32), grad_xn2)
    grad_hidden1 = cotangent.astype(jnp.float32) + grad_h1_norm
    grad_gain2 = jnp.sum(gain2_terms, axis=0)
    grad_branch = grad_hidden1.astype(jnp.bfloat16)
    grad_w_out = outer(mixed, grad_branch)
    grad_mixed = project(grad_branch, wo).reshape(rows, heads, head)
    grad_att = (grad_mixed * gates[:, :, None]).astype(jnp.bfloat16)
    grad_logits = (jnp.sum(grad_mixed * attended, axis=-1) * gates * (1.0 - gates)).astype(
        jnp.bfloat16
    )
    grad_blocks = grad_att.reshape(rows, pairs, pair, group, head).transpose(1, 2, 3, 0, 4)

    def backward_block(index):
        key_block = lax.dynamic_slice_in_dim(keys_all, index * pair * head, pair * head, 1).reshape(
            length, pair, head
        )
        value_block = lax.dynamic_slice_in_dim(
            values_all, index * pair * head, pair * head, 1
        ).reshape(length, pair, head)
        query_block = query_blocks[index]
        grad_out = grad_blocks[index]
        scores = block_scores(query_block, key_block, allowed, factor)
        probs = jnp.exp(scores - lse_blocks[index])
        grad_probs = jnp.einsum(
            "hgtd,khd->hgtk", grad_out, value_block, preferred_element_type=jnp.float32
        )
        delta = jnp.sum(probs * grad_probs, axis=-1, keepdims=True)
        grad_scores = (probs * (grad_probs - delta)).astype(jnp.bfloat16)
        grad_query = (
            jnp.einsum("hgtk,khd->hgtd", grad_scores, key_block, preferred_element_type=jnp.float32)
            * factor
        )
        grad_key = (
            jnp.einsum(
                "hgtk,hgtd->khd", grad_scores, query_block, preferred_element_type=jnp.float32
            )
            * factor
        )
        grad_value = jnp.einsum(
            "hgtk,hgtd->khd",
            probs.astype(jnp.bfloat16),
            grad_out,
            preferred_element_type=jnp.float32,
        )
        return (grad_query, grad_key, grad_value)

    grad_query_blocks, grad_key_all, grad_value_all = lax.map(backward_block, jnp.arange(pairs))
    grad_key_sum, grad_value_sum = (
        lax.psum_scatter(
            grad_key_all.astype(jnp.bfloat16), "ctx", scatter_dimension=1, tiled=True
        ).astype(jnp.float32),
        lax.psum_scatter(
            grad_value_all.astype(jnp.bfloat16), "ctx", scatter_dimension=1, tiled=True
        ).astype(jnp.float32),
    )
    grad_value_rows = (
        grad_value_sum.astype(jnp.bfloat16).transpose(1, 0, 2, 3).reshape(rows, kv_heads * head)
    )
    grad_key_rot = (
        grad_key_sum.astype(jnp.bfloat16)
        .astype(jnp.float32)
        .transpose(1, 0, 2, 3)
        .reshape(rows, kv_heads, head)
    )
    grad_key_normed = rotate(grad_key_rot, mine, -1.0)
    grad_key_pre, key_gain_terms = norm_back(
        key, key_scale, gk.astype(jnp.float32), grad_key_normed
    )
    grad_key_rows = grad_key_pre.astype(jnp.bfloat16).reshape(rows, kv_heads * head)
    grad_key_gain = jnp.sum(key_gain_terms, axis=(0, 1))
    grad_query_rot = (
        grad_query_blocks.transpose(3, 0, 1, 2, 4)
        .reshape(rows, heads, head)
        .astype(jnp.bfloat16)
        .astype(jnp.float32)
    )
    grad_query_normed = rotate(grad_query_rot, mine, -1.0)
    grad_query_pre, query_gain_terms = norm_back(
        query, query_scale, gq.astype(jnp.float32), grad_query_normed
    )
    grad_query_rows = grad_query_pre.astype(jnp.bfloat16).reshape(rows, heads * head)
    grad_query_gain = jnp.sum(query_gain_terms, axis=(0, 1))
    grad_w_query = outer(grad_query_rows, xn1)
    grad_w_key = outer(grad_key_rows, xn1)
    grad_w_value = outer(grad_value_rows, xn1)
    grad_w_headgate = outer(grad_logits, xn1)
    grad_xn1 = jnp.dot(grad_query_rows, wq, preferred_element_type=jnp.float32) + jnp.dot(
        grad_key_rows, wk, preferred_element_type=jnp.float32
    )
    grad_xn1 = (
        grad_xn1
        + jnp.dot(grad_value_rows, wv, preferred_element_type=jnp.float32)
        + jnp.dot(grad_logits, wgt, preferred_element_type=jnp.float32)
    )
    grad_x_norm, gain1_terms = norm_back(x, scale1, g1.astype(jnp.float32), grad_xn1)
    grad_tokens = grad_hidden1 + grad_x_norm
    grad_gain1 = jnp.sum(gain1_terms, axis=0)
    summed = (
        lax.psum_scatter(grad_w_query, ("seq", "ctx"), scatter_dimension=0, tiled=True),
        lax.psum_scatter(grad_w_key, ("seq", "ctx"), scatter_dimension=0, tiled=True),
        lax.psum_scatter(grad_w_value, ("seq", "ctx"), scatter_dimension=0, tiled=True),
        lax.psum_scatter(grad_w_out, ("seq", "ctx"), scatter_dimension=0, tiled=True),
        lax.psum_scatter(grad_w_headgate, ("seq", "ctx"), scatter_dimension=1, tiled=True),
        lax.psum_scatter(grad_gain1, ("seq", "ctx"), scatter_dimension=0, tiled=True),
        lax.psum_scatter(grad_query_gain, ("seq", "ctx"), scatter_dimension=0, tiled=True),
        lax.psum_scatter(grad_key_gain, ("seq", "ctx"), scatter_dimension=0, tiled=True),
        lax.psum_scatter(grad_gain2, ("seq", "ctx"), scatter_dimension=0, tiled=True),
    )
    g_wq, g_wk, g_wv, g_wo, g_wgt, g_g1, g_gq, g_gk, g_g2 = summed
    return (
        output,
        grad_tokens,
        g_wq,
        g_wk,
        g_wv,
        g_wo,
        g_wgt,
        g_g1,
        g_gq,
        g_gk,
        g_g2,
        grad_w_gate,
        grad_w_up,
        grad_w_down,
    )


BF16 = jnp.bfloat16
F32 = jnp.float32
BOTH = ("seq", "ctx")
ROWS = ((0,), (0,))
LAST = ((1,), (1,))


def swap(v, d):
    return lax.ppermute(v, "ctx", [(c, c ^ d) for c in range(8)])


def hop(v, d):
    return lax.ppermute(v, BOTH, [(i, i ^ d) for i in range(32)])


def turn(v):
    pairs = [
        (8 * r + 4 * q + j, 8 * j + 4 * q + r) for r in range(4) for q in range(2) for j in range(4)
    ]
    return lax.ppermute(v, BOTH, pairs)


def after(v, *others):
    return lax.optimization_barrier((v, *others))[0]


def gather_ctx(own):
    inner = [(c, c ^ 6) for c in range(8) if (c >> 1) in (1, 2)]
    outward = [(c, c ^ 2) for c in range(8) if (c >> 1) in (1, 2)]
    z = lax.axis_index("ctx") >> 1
    inside = (z == 1) | (z == 2)
    z1 = swap(own, 2)
    across = lax.ppermute(own, "ctx", inner)
    y0 = swap(own, 1)
    relayed = lax.ppermute(z1, "ctx", inner)
    outer_near = lax.ppermute(across, "ctx", outward)
    y1 = swap(z1, 1)
    outer_far = lax.ppermute(relayed, "ctx", outward)
    z2 = jnp.where(inside, relayed, outer_near)
    y2 = swap(z2, 1)
    z3 = jnp.where(inside, across, outer_far)
    y3 = swap(z3, 1)
    return [own, y0, z1, y1, z2, y2, z3, y3]


def scatter_ctx(blocks):
    other = [swap(blocks[2 * dz + 1], 1) for dz in range(4)]
    kept3 = (blocks[6].astype(F32) + other[3].astype(F32)).astype(BF16)
    far3 = swap(kept3, 4)
    kept2 = (blocks[4].astype(F32) + after(other[2], kept3).astype(F32)).astype(BF16)
    far2 = swap(kept2, 4)
    kept1 = blocks[2].astype(F32) + other[1].astype(F32)
    near = swap((kept1 + after(far3, kept2).astype(F32)).astype(BF16), 2)
    kept0 = blocks[0].astype(F32) + other[0].astype(F32)
    return kept0 + far2.astype(F32) + near.astype(F32)


def picked(v, c):
    v = v.reshape(8, v.shape[0] // 8, v.shape[1])
    return [lax.dynamic_index_in_dim(v, c ^ d, 0, keepdims=False) for d in range(8)]


def gather_small(v, flat):
    blocks = v
    for b in (2, 1, 0, 3, 4):
        other = hop(blocks, 1 << b)
        high = ((flat >> b) & 1) == 1
        blocks = jnp.where(high, jnp.stack([other, blocks]), jnp.stack([blocks, other]))
    return blocks.transpose((0, 1, 4, 3, 2, 5, 6)).reshape((32,) + v.shape)


def sum_small(v):
    for b in (0, 1, 2, 3, 4):
        v = v + hop(v, 1 << b)
    return v


def dot(left, right, dims):
    return lax.dot_general(left, right, (dims, ((), ())), preferred_element_type=F32)


def full(shape, **kw):
    return pl.BlockSpec(shape, lambda *_: (0,) * len(shape), **kw)


def call(kernel, *rest, **kw):
    inner = kernel_call(kernel, *rest, **kw)

    return inner


def kernel_call(kernel, grid, in_specs, out_specs, out_shape, flops, moved, exps=0, scratch=()):
    return pl.pallas_call(
        kernel,
        grid_spec=pltpu.PrefetchScalarGridSpec(
            num_scalar_prefetch=1,
            grid=grid,
            in_specs=in_specs,
            out_specs=out_specs,
            scratch_shapes=list(scratch),
        ),
        out_shape=out_shape,
        cost_estimate=pl.CostEstimate(flops=flops, bytes_accessed=moved, transcendentals=exps),
    )


def struct(shape, dtype):
    return jax.ShapeDtypeStruct(shape, dtype)


def projection_kernel(c_ref, *refs):
    chunks = refs[:8]
    packed = refs[8:12]
    wgt, g1, gq, gk, cosine, sine = refs[12:18]
    x_out, xn_out, q_out, k_out, v_out, qr_out, kr_out, gate_out, weights = refs[18:27]
    block = refs[27]
    d = pl.program_id(0)

    @pl.when(d == 0)
    def _():
        for e in range(4):
            j = c_ref[1] ^ e
            for start, size, first in ((0, 64, 0), (256, 32, 64), (384, 32, 96)):
                at = pl.multiple_of(start + size * j, size)
                weights[pl.ds(at, size)] = packed[e][first : first + size]

    for i in range(8):

        @pl.when(d == i)
        def _():
            block[...] = chunks[i][...]

    x_out[...] = block[...]
    x = block[...].astype(F32)
    xn = (x * lax.rsqrt(jnp.mean(x * x, axis=-1, keepdims=True) + EPS) * g1[...]).astype(BF16)
    xn_out[...] = xn
    made = dot(xn, weights[...], LAST)
    gate_out[...] = jax.nn.sigmoid(dot(xn, wgt[...], LAST))
    q_out[...] = made[:, :256]
    k_out[...] = made[:, 256:384]
    v_out[...] = made[:, 384:].astype(BF16)

    def turned(v, gain):
        v = v * lax.rsqrt(jnp.mean(v * v, axis=-1, keepdims=True) + EPS) * gain
        return (v * cosine[...] + pltpu.roll(v, HD // 2, 1) * sine[...]).astype(BF16)

    qr_out[:, :HD] = turned(made[:, :HD], gq[...])
    qr_out[:, HD:] = turned(made[:, HD : 2 * HD], gq[...])
    kr_out[...] = turned(made[:, 2 * HD : 3 * HD], gk[...])


def projection(c, chunks, packed, wgt, g1, gq, gk, cosine, sine):
    rows, width = chunks[0].shape
    length = 8 * rows
    at = lambda d, c: (c[0] ^ d, 0)
    return call(
        projection_kernel,
        (8,),
        [full((rows, width), pipeline_mode=pl.Buffered(1))] * 8
        + [
            *[full((128, width), pipeline_mode=pl.Buffered(1))] * 4,
            full(wgt.shape),
            full((1, width)),
            full((1, HD)),
            full((1, HD)),
            pl.BlockSpec((rows, HD), at),
            pl.BlockSpec((rows, HD), at),
        ],
        [
            *(pl.BlockSpec((rows, n), at) for n in (width, width, 2 * HD, HD, HD, 2 * HD, HD, 16)),
            full((512, width)),
        ],
        [
            struct((length, width), BF16),
            struct((length, width), BF16),
            struct((length, 2 * HD), F32),
            struct((length, HD), F32),
            struct((length, HD), BF16),
            struct((length, 2 * HD), BF16),
            struct((length, HD), BF16),
            struct((length, 16), F32),
            struct((512, width), BF16),
        ],
        2 * length * width * 528,
        20 * length * width,
        scratch=[pltpu.VMEM((rows, width), BF16)],
    )(c, *chunks, *packed, wgt, g1, gq, gk, cosine, sine)


def head_column(ref):
    value = ref[...]
    return jnp.where(pl.program_id(0) == 0, value[:, 0:1], value[:, 1:2])


def attention_kernel(
    c_ref, limit_ref, pos_ref, q_ref, k_ref, v_ref, gate_ref, out_ref, mixed_ref, lse_ref
):
    scores = dot(q_ref[...], k_ref[...], LAST) * (HD**-0.5)
    scores = jnp.where(pos_ref[...] <= limit_ref[...], scores, NEG)
    top = jnp.max(scores, axis=-1, keepdims=True)
    weights = jnp.exp(scores - top)
    total = jnp.sum(weights, axis=-1, keepdims=True)
    probs = (weights * (1.0 / total)).astype(BF16)
    attended = jnp.dot(probs, v_ref[...], preferred_element_type=F32)
    out_ref[...] = attended
    mixed_ref[...] = (attended * head_column(gate_ref)).astype(BF16)
    lse_ref[0] = top + jnp.log(total)


def attention(c, q, k, v, gates, limit, pos, tile=256):
    length = q.shape[0]
    return call(
        attention_kernel,
        (2, length // tile),
        [
            pl.BlockSpec((tile, 1), lambda h, i, c: (i, 0)),
            full((1, length)),
            pl.BlockSpec((tile, HD), lambda h, i, c: (i, h)),
            full((length, HD)),
            full((length, HD)),
            pl.BlockSpec((tile, 16), lambda h, i, c: (i, 0)),
        ],
        [
            pl.BlockSpec((tile, HD), lambda h, i, c: (i, h)),
            pl.BlockSpec((tile, HD), lambda h, i, c: (i, h)),
            pl.BlockSpec((1, tile, 1), lambda h, i, c: (h, i, 0)),
        ],
        [
            struct((length, 2 * HD), F32),
            struct((length, 2 * HD), BF16),
            struct((2, length, 1), F32),
        ],
        8 * length * length * HD,
        16 * length * HD,
        2 * length * length,
    )(c, limit, pos, q, k, v, gates)


def hidden_kernel(c_ref, *refs):
    mixed = refs[:8]
    x, wo, g2 = refs[8:11]
    xn_out, own_out = refs[11:13]
    total = refs[13]
    i = pl.program_id(0)
    c = c_ref[0]
    total[...] = x[...].astype(F32)
    for d in range(8):
        other = c ^ d
        total[...] += jnp.dot(
            mixed[d][...], wo[2 * (other & 3) + (other >> 2)], preferred_element_type=F32
        )
    h = total[...]
    xn_out[...] = (
        h * lax.rsqrt(jnp.mean(h * h, axis=-1, keepdims=True) + EPS) * g2[...]
    ).astype(BF16)

    @pl.when(i == c >> 1)
    def _():
        own_out[...] = total[pl.ds((c & 1) * 128, 128)]


def hidden(c, mixed, x_all, wo, g2):
    length, width = x_all.shape
    return call(
        hidden_kernel,
        (4,),
        [pl.BlockSpec((256, 256), lambda i, c: (i, 0))] * 8
        + [
            pl.BlockSpec((256, width), lambda i, c: (i, 0)),
            full((8, 256, width), pipeline_mode=pl.Buffered(1)),
            full((1, width)),
        ],
        [pl.BlockSpec((256, width), lambda i, c: (i, 0)), full((128, width))],
        [struct((length, width), BF16), struct((128, width), F32)],
        2 * length * width * width,
        12 * length * width,
        scratch=[pltpu.VMEM((256, width), F32)],
    )(c, *mixed, x_all, wo.reshape(8, 256, width), g2)


def join_kernel(c_ref, *refs):
    for i in range(8):

        @pl.when(pl.program_id(0) == i)
        def _():
            refs[8][...] = refs[i][...]


def join(c, chunks):
    rows, width = chunks[0].shape
    return call(
        join_kernel,
        (8,),
        [full((rows, width), pipeline_mode=pl.Buffered(1))] * 8,
        pl.BlockSpec((rows, width), lambda d, c: (c[0] ^ d, 0)),
        struct((8 * rows, width), chunks[0].dtype),
        0,
        32 * rows * width,
    )(c, *chunks)


def mixed_back_kernel(c_ref, *refs):
    chunks = refs[:8]
    wo, attended, gate_ref = refs[8:11]
    all_out, att_out, logit_out = refs[11:]
    for i in range(8):

        @pl.when(pl.program_id(0) == i)
        def _():
            all_out[...] = chunks[i][...]

    grad = dot(all_out[...], wo[0], LAST)
    gates = gate_ref[...]
    lane = lax.broadcasted_iota(jnp.int32, gates.shape, 1)
    logits = jnp.zeros_like(gates)
    for h in range(2):
        part = grad[:, h * HD : (h + 1) * HD]
        gate = gates[:, h : h + 1]
        att_out[:, h * HD : (h + 1) * HD] = (part * gate).astype(BF16)
        along = jnp.sum(part * attended[:, h * HD : (h + 1) * HD], axis=-1, keepdims=True)
        logits = jnp.where(lane == h, along * gate * (1.0 - gate), logits)
    logit_out[...] = logits.astype(BF16)


def mixed_back(c, chunks, wo, attended, gates):
    rows, width = chunks[0].shape
    length = 8 * rows
    at = lambda d, c: (c[0] ^ d, 0)
    return call(
        mixed_back_kernel,
        (8,),
        [full((rows, width), pipeline_mode=pl.Buffered(1))] * 8
        + [
            pl.BlockSpec((1, 256, width), lambda d, c: (2 * (c[0] & 3) + (c[0] >> 2), 0, 0)),
            pl.BlockSpec((rows, 256), at),
            pl.BlockSpec((rows, 16), at),
        ],
        [pl.BlockSpec((rows, n), at) for n in (width, 256, 16)],
        [struct((length, n), BF16) for n in (width, 256, 16)],
        512 * length * width,
        6 * length * width,
    )(c, *chunks, wo.reshape(8, 256, width), attended, gates)


def attention_back_kernel(c_ref, *refs):
    limit_ref, pos_ref, qr, kr, v, lse_ref, g, q_pre, k_pre, cosine, sine, cosine_all, sine_all = refs[:13]
    gq, gk = refs[13:15]
    gq_out, gk_out, gv_out, gains_out = refs[15:19]
    gk_sum, gv_sum = refs[19:]
    first = (pl.program_id(0) == 0) & (pl.program_id(1) == 0)
    last = (pl.program_id(0) == 1) & (pl.program_id(1) == pl.num_programs(1) - 1)

    def back(rotated, pre, gain, cos_ref, sin_ref):
        grad = rotated.astype(BF16).astype(F32)
        grad = grad * cos_ref[...] - pltpu.roll(grad, HD // 2, 1) * sin_ref[...]
        scale = lax.rsqrt(jnp.mean(pre * pre, axis=-1, keepdims=True) + EPS)
        weighted = grad * gain
        out = scale * weighted - pre * (scale * scale * scale) * jnp.mean(
            weighted * pre, axis=-1, keepdims=True
        )
        return out.astype(BF16), jnp.sum(grad * pre * scale, axis=0, keepdims=True)

    @pl.when(first)
    def _():
        gk_sum[...] = jnp.zeros_like(gk_sum)
        gv_sum[...] = jnp.zeros_like(gv_sum)
        gains_out[...] = jnp.zeros_like(gains_out)

    scores = dot(qr[...], kr[...], LAST) * (HD**-0.5)
    scores = jnp.where(pos_ref[...] <= limit_ref[...], scores, NEG)
    probs = jnp.exp(scores - lse_ref[0])
    grad_probs = dot(g[...], v[...], LAST)
    delta = jnp.sum(probs * grad_probs, axis=-1, keepdims=True)
    grad_scores = (probs * (grad_probs - delta)).astype(BF16)
    rotated = jnp.dot(grad_scores, kr[...], preferred_element_type=F32) * (HD**-0.5)
    gk_sum[...] += dot(grad_scores, qr[...], ROWS)
    gv_sum[...] += dot(probs.astype(BF16), g[...], ROWS)
    gq_out[...], terms = back(rotated, q_pre[...], gq[...], cosine, sine)
    gains_out[0:1] += terms

    @pl.when(last)
    def _():
        gk_out[...], key_terms = back(
            gk_sum[...] * (HD**-0.5), k_pre[...], gk[...], cosine_all, sine_all
        )
        gains_out[1:2] += key_terms
        gv_out[...] = gv_sum[...].astype(BF16)


def attention_back(c, qr, kr, v, lse, grad, q_pre, k_pre, cosine, sine, gq, gk, limit, pos, tile=256):
    length = qr.shape[0]
    mine = pl.BlockSpec((tile, HD), lambda h, i, c: (i, h))
    rows = pl.BlockSpec((tile, HD), lambda h, i, c: (i, 0))
    whole = full((length, HD))
    return call(
        attention_back_kernel,
        (2, length // tile),
        [
            pl.BlockSpec((tile, 1), lambda h, i, c: (i, 0)),
            full((1, length)),
            mine,
            whole,
            whole,
            pl.BlockSpec((1, tile, 1), lambda h, i, c: (h, i, 0)),
            mine,
            mine,
            whole,
            rows,
            rows,
            whole,
            whole,
            full((1, HD)),
            full((1, HD)),
        ],
        [mine, whole, whole, full((8, HD))],
        [
            struct((length, 2 * HD), BF16),
            struct((length, HD), BF16),
            struct((length, HD), BF16),
            struct((8, HD), F32),
        ],
        20 * length * length * HD,
        40 * length * HD,
        2 * length * length,
        scratch=[pltpu.VMEM((length, HD), F32), pltpu.VMEM((length, HD), F32)],
    )(c, limit, pos, qr, kr, v, lse, grad, q_pre, k_pre, cosine, sine, cosine, sine, gq, gk)


def input_back_kernel(c_ref, *refs):
    gq, gk, gv, logits, weights, wgt, xn, g1, gain2, heads = refs[:10]
    outs = refs[10:18]
    bundle, gate_sum = refs[18:]
    d = pl.program_id(0)
    mine = 2 * (c_ref[0] & 3) + (c_ref[0] >> 2)

    @pl.when(d == 0)
    def _():
        bundle[...] = jnp.zeros_like(bundle)
        gate_sum[...] = jnp.zeros_like(gate_sum)

    part = jnp.dot(gq[...], weights[:256], preferred_element_type=F32)
    part += jnp.dot(
        jnp.concatenate([gk[...], gv[...]], axis=1), weights[256:], preferred_element_type=F32
    )
    part += jnp.dot(logits[...], wgt[...], preferred_element_type=F32)
    bundle[16:17] += jnp.sum(part * xn[...].astype(F32), axis=0, keepdims=True)
    gate_sum[...] += dot(logits[...], xn[...], ROWS)
    for i in range(8):

        @pl.when(d == i)
        def _():
            outs[i][...] = part.astype(BF16)

    @pl.when(d == 7)
    def _():
        bundle[16:17] = bundle[16:17] / g1[...]
        bundle[17:18] = gain2[...]
        bundle[18:19, :HD] = heads[0:1]
        bundle[18:19, HD : 2 * HD] = heads[1:2]
        for g in range(8):

            @pl.when(mine == g)
            def _():
                bundle[2 * g : 2 * g + 2] = gate_sum[0:2]


def input_back(c, gq, gk, gv, logits, weights, wgt, xn, g1, gain2, heads):
    length, width = xn.shape
    rows = length // 8
    at = lambda d, c: (c[0] ^ d, 0)
    return call(
        input_back_kernel,
        (8,),
        [pl.BlockSpec((rows, n), at) for n in (256, HD, HD, 16)]
        + [
            full(weights.shape, pipeline_mode=pl.Buffered(1)),
            full(wgt.shape),
            pl.BlockSpec((rows, width), at),
            full((1, width)),
            full((1, width)),
            full((8, HD)),
        ],
        [full((rows, width))] * 8 + [full((24, width))],
        [struct((rows, width), BF16)] * 8 + [struct((24, width), F32)],
        1056 * length * width,
        8 * length * width,
        scratch=[pltpu.VMEM((16, width), F32)],
    )(c, gq, gk, gv, logits, weights, wgt, xn, g1, gain2, heads)


def per_device_small(*args):
    return layer_small(*args)


def layer_small(
    tokens,
    prefix,
    span_order,
    w_query,
    w_key,
    w_value,
    w_out,
    w_headgate,
    attn_gain,
    query_gain,
    key_gain,
    mlp_gain,
    w_gate,
    w_up,
    w_down,
    cotangent,
):
    rows, width = tokens.shape
    length = 8 * rows
    span = rows // 2
    s = lax.axis_index("seq")
    c = lax.axis_index("ctx")
    flat = 8 * s + c
    mine = 2 * (c & 3) + (c >> 2)
    cs = jnp.stack([c, s]).astype(jnp.int32)

    small = jnp.concatenate(
        [
            w_headgate,
            attn_gain[None],
            mlp_gain[None],
            jnp.pad(jnp.concatenate([query_gain, key_gain]), (0, 56))[None],
            jnp.zeros((13, 64), BF16),
        ],
        axis=0,
    )
    smalls = gather_small(small, flat)
    wgt = smalls[:, :16].transpose(1, 0, 2).reshape(H, width)
    wgt = lax.dynamic_slice_in_dim(jnp.concatenate([wgt, wgt], 0), 2 * mine, 16, 0)
    g1 = smalls[:, 16].reshape(1, width).astype(F32)
    g2 = smalls[:, 17].reshape(1, width).astype(F32)
    gq = smalls[:, 18, :4].reshape(1, HD).astype(F32)
    gk = smalls[:, 18, 4:8].reshape(1, HD).astype(F32)

    x_chunks = gather_ctx(tokens)
    local = jnp.concatenate([w_query, w_key, w_value], axis=0)
    packed = [turn(local)]
    packed.append(hop(packed[0], 8))
    packed.append(hop(packed[0], 16))
    packed.append(hop(packed[2], 8))
    wo = lax.all_gather(w_out, BOTH, axis=0, tiled=True)
    wd = lax.all_gather(w_down, "seq", axis=0, tiled=True)
    wg = lax.all_gather(w_gate, "seq", axis=0, tiled=True)
    wu = lax.all_gather(w_up, "seq", axis=0, tiled=True)

    pos = (span_order[0][:, None] * span + jnp.arange(span, dtype=jnp.int32)).reshape(length)
    limit = jnp.maximum(pos, prefix[0] - 1)
    half = HD // 2
    inv_freq = 1.0 / ROPE_BASE ** (jnp.arange(half, dtype=F32) * 2.0 / HD)
    angles = pos.astype(F32)[:, None] * inv_freq[None, :]
    cosine = jnp.cos(angles)
    sine = jnp.sin(angles)
    cosine = jnp.concatenate([cosine, cosine], axis=1)
    sine = jnp.concatenate([-sine, sine], axis=1)
    limit = limit[:, None]
    pos = pos[None, :]

    x_all, xn1, q_pre, k_pre, value, qr, kr, gates, w_qkv = projection(
        cs, x_chunks, packed, wgt, g1, gq, gk, cosine, sine
    )
    cot_chunks = gather_ctx(after(cotangent, *x_chunks))
    attended, mixed, lse = attention(cs, qr, kr, value, gates, limit, pos)
    mixed_chunks = gather_ctx(mixed)
    xn2_all, hidden1 = hidden(cs, mixed_chunks, x_all, wo, g2)
    cot_all = join(cs, cot_chunks)

    gate = project(xn2_all, wg)
    up = project(xn2_all, wu)
    grad_act = project(cot_all, wd)
    sig = jax.nn.sigmoid(gate)
    silu = gate * sig
    act = (silu * up).astype(BF16)
    grad_gate = (grad_act * up * sig * (1.0 + gate * (1.0 - sig))).astype(BF16)
    grad_up = (grad_act * silu).astype(BF16)
    grad_xn2_part = (
        jnp.dot(grad_gate, wg, preferred_element_type=F32)
        + jnp.dot(grad_up, wu, preferred_element_type=F32)
    ).astype(BF16)
    grad_xn2 = scatter_ctx(picked(grad_xn2_part, c))
    ff_grads = [
        outer(left, right).astype(BF16)
        for left, right in ((grad_gate, xn2_all), (grad_up, xn2_all), (act, cot_all))
    ]
    grad_w_gate, grad_w_up, grad_w_down = (
        lax.psum_scatter(v, "seq", scatter_dimension=0, tiled=True).astype(F32)
        for v in ff_grads
    )
    branch_part = jnp.dot(act, wd, preferred_element_type=F32).astype(BF16)

    _, scale2 = norm_apply(hidden1, g2)
    grad_h1_norm, gain2_terms = norm_back(hidden1, scale2, g2, grad_xn2)
    grad_hidden1 = cotangent.astype(F32) + grad_h1_norm
    grad_gain2 = jnp.sum(gain2_terms, axis=0)
    branch_chunks = gather_ctx(after(grad_hidden1.astype(BF16), *ff_grads, branch_part))
    grad_branch_all, grad_att, grad_logits = mixed_back(cs, branch_chunks, wo, attended, gates)
    branch = scatter_ctx(picked(after(branch_part, *branch_chunks), c))
    output = (hidden1 + branch).astype(BF16)

    gq_rows, gk_rows, gv_rows, head_gains = attention_back(
        cs, qr, kr, value, lse, grad_att, q_pre, k_pre, cosine, sine, gq, gk, limit, pos
    )
    *parts, bundle = input_back(
        cs, gq_rows, gk_rows, gv_rows, grad_logits, w_qkv, wgt, xn1, g1, grad_gain2[None], head_gains
    )
    grad_xn1 = scatter_ctx(parts)
    x = tokens.astype(F32)
    scale1 = lax.rsqrt(jnp.mean(x * x, axis=-1, keepdims=True) + EPS)
    grad_x, _ = norm_back(x, scale1, g1, grad_xn1)
    grad_tokens = grad_hidden1 + grad_x

    pieces = jnp.concatenate(
        [
            outer(gq_rows, xn1).astype(BF16).reshape(4, 64, width),
            outer(gk_rows, xn1).astype(BF16).reshape(4, 32, width),
            outer(gv_rows, xn1).astype(BF16).reshape(4, 32, width),
            outer(mixed, grad_branch_all).astype(BF16).reshape(4, 64, width),
        ],
        axis=1,
    ).reshape(4 * 192, width)
    home = lax.psum_scatter(pieces, "seq", scatter_dimension=0, tiled=True)
    home = turn(home).astype(F32)
    g_wq, g_wk, g_wv, g_wo = home[:64], home[64:96], home[96:128], home[128:]

    bundle = sum_small(bundle)
    blocks = lax.dynamic_slice_in_dim(bundle[:18], 64 * flat, 64, 1)
    heads = lax.dynamic_slice_in_dim(bundle[18, : 2 * HD].reshape(2, HD), 4 * flat, 4, 1)
    return (
        output,
        grad_tokens,
        g_wq,
        g_wk,
        g_wv,
        g_wo,
        blocks[:16],
        blocks[16],
        heads[0],
        heads[1],
        blocks[17],
        grad_w_gate,
        grad_w_up,
        grad_w_down,
    )


def solution(mesh):
    in_specs = (
        P(("seq", "ctx"), None),
        P("seq"),
        P("seq", None),
        P(("seq", "ctx"), None),
        P(("seq", "ctx"), None),
        P(("seq", "ctx"), None),
        P(("seq", "ctx"), None),
        P(None, ("seq", "ctx")),
        P(("seq", "ctx")),
        P(("seq", "ctx")),
        P(("seq", "ctx")),
        P(("seq", "ctx")),
        P(("seq", "ctx"), None),
        P(("seq", "ctx"), None),
        P(("seq", "ctx"), None),
        P(("seq", "ctx"), None),
    )
    out_specs = (
        P(("seq", "ctx"), None),
        P(("seq", "ctx"), None),
        P(("seq", "ctx"), None),
        P(("seq", "ctx"), None),
        P(("seq", "ctx"), None),
        P(("seq", "ctx"), None),
        P(None, ("seq", "ctx")),
        P(("seq", "ctx")),
        P(("seq", "ctx")),
        P(("seq", "ctx")),
        P(("seq", "ctx")),
        P(("seq", "ctx"), None),
        P(("seq", "ctx"), None),
        P(("seq", "ctx"), None),
    )
    sizes = dict(mesh.shape)
    small = sizes == {"seq": 4, "ctx": 8}
    return jax.shard_map(
        per_device_small if small else per_device, mesh=mesh, in_specs=in_specs, out_specs=out_specs, check_vma=False
    )
```

```python
import jax
import jax.numpy as jnp
from jax import lax
from jax.experimental import pallas as pl
from jax.experimental.pallas import tpu as pltpu

from jax.sharding import PartitionSpec as P

H = 16
KVH = 8
HD = 128


EPS = 1e-06
ROPE_BASE = 1000000.0
NEG = -1e30


def rotate(v, positions, sign):
    half = v.shape[-1] // 2
    inv_freq = 1.0 / ROPE_BASE ** (jnp.arange(half, dtype=jnp.float32) * 2.0 / v.shape[-1])
    angles = positions.astype(jnp.float32)[:, None] * inv_freq[None, :]
    cosine = jnp.cos(angles)[:, None, :]
    sine = sign * jnp.sin(angles)[:, None, :]
    first = v[..., :half]
    second = v[..., half:]
    return jnp.concatenate(
        [first * cosine - second * sine, second * cosine + first * sine], axis=-1
    )


def norm_apply(v, gain):
    factor = lax.rsqrt(jnp.mean(v * v, axis=-1, keepdims=True) + EPS)
    return (v * factor * gain, factor)


def norm_back(v, factor, gain, grad):
    weighted = grad * gain
    grad_v = factor * weighted - v * (factor * factor * factor) * jnp.mean(
        weighted * v, axis=-1, keepdims=True
    )
    return (grad_v, grad * v * factor)


def project(left, right):
    return lax.dot_general(
        left, right, (((1,), (1,)), ((), ())), preferred_element_type=jnp.float32
    )


def outer(left, right):
    return lax.dot_general(
        left, right, (((0,), (0,)), ((), ())), preferred_element_type=jnp.float32
    )


def block_scores(query_block, key_block, allowed, factor):
    scores = (
        jnp.einsum("hgtd,khd->hgtk", query_block, key_block, preferred_element_type=jnp.float32)
        * factor
    )
    return jnp.where(allowed[None, None], scores, NEG)


def per_device(
    tokens,
    prefix,
    span_order,
    w_query,
    w_key,
    w_value,
    w_out,
    w_headgate,
    attn_gain,
    query_gain,
    key_gain,
    mlp_gain,
    w_gate,
    w_up,
    w_down,
    cotangent,
):
    rows = tokens.shape[0]
    span = rows // 2
    length = rows * lax.axis_size("ctx")
    heads = H
    kv_heads = KVH
    head = HD
    group = heads // kv_heads
    pair = 2
    pairs = kv_heads // pair
    factor = head ** (-0.5)
    order = span_order[0]
    offsets = jnp.arange(span, dtype=jnp.int32)
    every_pos = (order[:, None] * span + offsets[None, :]).reshape(length)
    mine = lax.dynamic_slice_in_dim(every_pos, lax.axis_index("ctx") * rows, rows)
    limit = jnp.maximum(mine, prefix[0] - 1)
    allowed = every_pos[None, :] <= limit[:, None]
    wq, wk, wv, wo, wgt, g1, gq, gk, g2 = (
        lax.all_gather(w_query, ("seq", "ctx"), axis=0, tiled=True),
        lax.all_gather(w_key, ("seq", "ctx"), axis=0, tiled=True),
        lax.all_gather(w_value, ("seq", "ctx"), axis=0, tiled=True),
        lax.all_gather(w_out, ("seq", "ctx"), axis=0, tiled=True),
        lax.all_gather(w_headgate, ("seq", "ctx"), axis=1, tiled=True),
        lax.all_gather(attn_gain, ("seq", "ctx"), axis=0, tiled=True),
        lax.all_gather(query_gain, ("seq", "ctx"), axis=0, tiled=True),
        lax.all_gather(key_gain, ("seq", "ctx"), axis=0, tiled=True),
        lax.all_gather(mlp_gain, ("seq", "ctx"), axis=0, tiled=True),
    )
    x = tokens.astype(jnp.float32)
    xn1_full, scale1 = norm_apply(x, g1.astype(jnp.float32))
    xn1 = xn1_full.astype(jnp.bfloat16)
    query = project(xn1, wq).reshape(rows, heads, head)
    key = project(xn1, wk).reshape(rows, kv_heads, head)
    value = project(xn1, wv).astype(jnp.bfloat16)
    logits = project(xn1, wgt)
    query_normed, query_scale = norm_apply(query, gq.astype(jnp.float32))
    key_normed, key_scale = norm_apply(key, gk.astype(jnp.float32))
    query_rot = rotate(query_normed, mine, 1.0).astype(jnp.bfloat16)
    key_rot = rotate(key_normed, mine, 1.0).astype(jnp.bfloat16).reshape(rows, kv_heads * head)
    keys_all, values_all = (
        lax.all_gather(key_rot, "ctx", axis=0, tiled=True),
        lax.all_gather(value, "ctx", axis=0, tiled=True),
    )
    query_blocks = query_rot.reshape(rows, pairs, pair, group, head).transpose(1, 2, 3, 0, 4)

    def forward_block(index):
        key_block = lax.dynamic_slice_in_dim(keys_all, index * pair * head, pair * head, 1).reshape(
            length, pair, head
        )
        value_block = lax.dynamic_slice_in_dim(
            values_all, index * pair * head, pair * head, 1
        ).reshape(length, pair, head)
        scores = block_scores(query_blocks[index], key_block, allowed, factor)
        lse = jax.nn.logsumexp(scores, axis=-1, keepdims=True)
        probs = jnp.exp(scores - lse).astype(jnp.bfloat16)
        return (
            jnp.einsum("hgtk,khd->hgtd", probs, value_block, preferred_element_type=jnp.float32),
            lse,
        )

    attended_blocks, lse_blocks = lax.map(forward_block, jnp.arange(pairs))
    attended = attended_blocks.transpose(3, 0, 1, 2, 4).reshape(rows, heads, head)
    gates = jax.nn.sigmoid(logits)
    mixed = (attended * gates[:, :, None]).reshape(rows, heads * head).astype(jnp.bfloat16)
    hidden1 = x + jnp.dot(mixed, wo, preferred_element_type=jnp.float32)
    xn2_full, scale2 = norm_apply(hidden1, g2.astype(jnp.float32))
    xn2 = xn2_full.astype(jnp.bfloat16)
    gate_local, up_local, down_local = (
        lax.all_gather(w_gate, "seq", axis=0, tiled=True),
        lax.all_gather(w_up, "seq", axis=0, tiled=True),
        lax.all_gather(w_down, "seq", axis=0, tiled=True),
    )
    xn2_all, grad_y_all = (
        lax.all_gather(xn2, "ctx", axis=0, tiled=True),
        lax.all_gather(cotangent, "ctx", axis=0, tiled=True),
    )
    gate_part = project(xn2_all, gate_local)
    up_part = project(xn2_all, up_local)
    act_part = (jax.nn.silu(gate_part) * up_part).astype(jnp.bfloat16)
    branch = lax.psum_scatter(
        jnp.dot(act_part, down_local, preferred_element_type=jnp.float32).astype(jnp.bfloat16),
        "ctx",
        scatter_dimension=0,
        tiled=True,
    ).astype(jnp.float32)
    output = (hidden1 + branch).astype(jnp.bfloat16)
    gate_all = project(xn2_all, gate_local)
    up_all = project(xn2_all, up_local)
    sig_all = jax.nn.sigmoid(gate_all)
    silu_all = gate_all * sig_all
    act_local = (silu_all * up_all).astype(jnp.bfloat16)
    grad_act_all = project(grad_y_all, down_local)
    grad_gate_local = (grad_act_all * up_all * sig_all * (1.0 + gate_all * (1.0 - sig_all))).astype(
        jnp.bfloat16
    )
    grad_up_local = (grad_act_all * silu_all).astype(jnp.bfloat16)
    grad_xn2 = lax.psum_scatter(
        (
            jnp.dot(grad_gate_local, gate_local, preferred_element_type=jnp.float32)
            + jnp.dot(grad_up_local, up_local, preferred_element_type=jnp.float32)
        ).astype(jnp.bfloat16),
        "ctx",
        scatter_dimension=0,
        tiled=True,
    ).astype(jnp.float32)
    grad_w_gate, grad_w_up, grad_w_down = (
        lax.psum_scatter(
            outer(grad_gate_local, xn2_all).astype(jnp.bfloat16),
            "seq",
            scatter_dimension=0,
            tiled=True,
        ).astype(jnp.float32),
        lax.psum_scatter(
            outer(grad_up_local, xn2_all).astype(jnp.bfloat16),
            "seq",
            scatter_dimension=0,
            tiled=True,
        ).astype(jnp.float32),
        lax.psum_scatter(
            outer(act_local, grad_y_all).astype(jnp.bfloat16),
            "seq",
            scatter_dimension=0,
            tiled=True,
        ).astype(jnp.float32),
    )
    grad_h1_norm, gain2_terms = norm_back(hidden1, scale2, g2.astype(jnp.float32), grad_xn2)
    grad_hidden1 = cotangent.astype(jnp.float32) + grad_h1_norm
    grad_gain2 = jnp.sum(gain2_terms, axis=0)
    grad_branch = grad_hidden1.astype(jnp.bfloat16)
    grad_w_out = outer(mixed, grad_branch)
    grad_mixed = project(grad_branch, wo).reshape(rows, heads, head)
    grad_att = (grad_mixed * gates[:, :, None]).astype(jnp.bfloat16)
    grad_logits = (jnp.sum(grad_mixed * attended, axis=-1) * gates * (1.0 - gates)).astype(
        jnp.bfloat16
    )
    grad_blocks = grad_att.reshape(rows, pairs, pair, group, head).transpose(1, 2, 3, 0, 4)

    def backward_block(index):
        key_block = lax.dynamic_slice_in_dim(keys_all, index * pair * head, pair * head, 1).reshape(
            length, pair, head
        )
        value_block = lax.dynamic_slice_in_dim(
            values_all, index * pair * head, pair * head, 1
        ).reshape(length, pair, head)
        query_block = query_blocks[index]
        grad_out = grad_blocks[index]
        scores = block_scores(query_block, key_block, allowed, factor)
        probs = jnp.exp(scores - lse_blocks[index])
        grad_probs = jnp.einsum(
            "hgtd,khd->hgtk", grad_out, value_block, preferred_element_type=jnp.float32
        )
        delta = jnp.sum(probs * grad_probs, axis=-1, keepdims=True)
        grad_scores = (probs * (grad_probs - delta)).astype(jnp.bfloat16)
        grad_query = (
            jnp.einsum("hgtk,khd->hgtd", grad_scores, key_block, preferred_element_type=jnp.float32)
            * factor
        )
        grad_key = (
            jnp.einsum(
                "hgtk,hgtd->khd", grad_scores, query_block, preferred_element_type=jnp.float32
            )
            * factor
        )
        grad_value = jnp.einsum(
            "hgtk,hgtd->khd",
            probs.astype(jnp.bfloat16),
            grad_out,
            preferred_element_type=jnp.float32,
        )
        return (grad_query, grad_key, grad_value)

    grad_query_blocks, grad_key_all, grad_value_all = lax.map(backward_block, jnp.arange(pairs))
    grad_key_sum, grad_value_sum = (
        lax.psum_scatter(
            grad_key_all.astype(jnp.bfloat16), "ctx", scatter_dimension=1, tiled=True
        ).astype(jnp.float32),
        lax.psum_scatter(
            grad_value_all.astype(jnp.bfloat16), "ctx", scatter_dimension=1, tiled=True
        ).astype(jnp.float32),
    )
    grad_value_rows = (
        grad_value_sum.astype(jnp.bfloat16).transpose(1, 0, 2, 3).reshape(rows, kv_heads * head)
    )
    grad_key_rot = (
        grad_key_sum.astype(jnp.bfloat16)
        .astype(jnp.float32)
        .transpose(1, 0, 2, 3)
        .reshape(rows, kv_heads, head)
    )
    grad_key_normed = rotate(grad_key_rot, mine, -1.0)
    grad_key_pre, key_gain_terms = norm_back(
        key, key_scale, gk.astype(jnp.float32), grad_key_normed
    )
    grad_key_rows = grad_key_pre.astype(jnp.bfloat16).reshape(rows, kv_heads * head)
    grad_key_gain = jnp.sum(key_gain_terms, axis=(0, 1))
    grad_query_rot = (
        grad_query_blocks.transpose(3, 0, 1, 2, 4)
        .reshape(rows, heads, head)
        .astype(jnp.bfloat16)
        .astype(jnp.float32)
    )
    grad_query_normed = rotate(grad_query_rot, mine, -1.0)
    grad_query_pre, query_gain_terms = norm_back(
        query, query_scale, gq.astype(jnp.float32), grad_query_normed
    )
    grad_query_rows = grad_query_pre.astype(jnp.bfloat16).reshape(rows, heads * head)
    grad_query_gain = jnp.sum(query_gain_terms, axis=(0, 1))
    grad_w_query = outer(grad_query_rows, xn1)
    grad_w_key = outer(grad_key_rows, xn1)
    grad_w_value = outer(grad_value_rows, xn1)
    grad_w_headgate = outer(grad_logits, xn1)
    grad_xn1 = jnp.dot(grad_query_rows, wq, preferred_element_type=jnp.float32) + jnp.dot(
        grad_key_rows, wk, preferred_element_type=jnp.float32
    )
    grad_xn1 = (
        grad_xn1
        + jnp.dot(grad_value_rows, wv, preferred_element_type=jnp.float32)
        + jnp.dot(grad_logits, wgt, preferred_element_type=jnp.float32)
    )
    grad_x_norm, gain1_terms = norm_back(x, scale1, g1.astype(jnp.float32), grad_xn1)
    grad_tokens = grad_hidden1 + grad_x_norm
    grad_gain1 = jnp.sum(gain1_terms, axis=0)
    summed = (
        lax.psum_scatter(grad_w_query, ("seq", "ctx"), scatter_dimension=0, tiled=True),
        lax.psum_scatter(grad_w_key, ("seq", "ctx"), scatter_dimension=0, tiled=True),
        lax.psum_scatter(grad_w_value, ("seq", "ctx"), scatter_dimension=0, tiled=True),
        lax.psum_scatter(grad_w_out, ("seq", "ctx"), scatter_dimension=0, tiled=True),
        lax.psum_scatter(grad_w_headgate, ("seq", "ctx"), scatter_dimension=1, tiled=True),
        lax.psum_scatter(grad_gain1, ("seq", "ctx"), scatter_dimension=0, tiled=True),
        lax.psum_scatter(grad_query_gain, ("seq", "ctx"), scatter_dimension=0, tiled=True),
        lax.psum_scatter(grad_key_gain, ("seq", "ctx"), scatter_dimension=0, tiled=True),
        lax.psum_scatter(grad_gain2, ("seq", "ctx"), scatter_dimension=0, tiled=True),
    )
    g_wq, g_wk, g_wv, g_wo, g_wgt, g_g1, g_gq, g_gk, g_g2 = summed
    return (
        output,
        grad_tokens,
        g_wq,
        g_wk,
        g_wv,
        g_wo,
        g_wgt,
        g_g1,
        g_gq,
        g_gk,
        g_g2,
        grad_w_gate,
        grad_w_up,
        grad_w_down,
    )


BF16 = jnp.bfloat16
F32 = jnp.float32
BOTH = ("seq", "ctx")
ROWS = ((0,), (0,))
LAST = ((1,), (1,))


def swap(v, d):
    return lax.ppermute(v, "ctx", [(c, c ^ d) for c in range(8)])


def hop(v, d):
    return lax.ppermute(v, BOTH, [(i, i ^ d) for i in range(32)])


def turn(v):
    pairs = [
        (8 * r + 4 * q + j, 8 * j + 4 * q + r) for r in range(4) for q in range(2) for j in range(4)
    ]
    return lax.ppermute(v, BOTH, pairs)


def after(v, *others):
    return lax.optimization_barrier((v, *others))[0]


def gather_ctx(own):
    inner = [(c, c ^ 6) for c in range(8) if (c >> 1) in (1, 2)]
    outward = [(c, c ^ 2) for c in range(8) if (c >> 1) in (1, 2)]
    z = lax.axis_index("ctx") >> 1
    inside = (z == 1) | (z == 2)
    z1 = swap(own, 2)
    across = lax.ppermute(own, "ctx", inner)
    y0 = swap(own, 1)
    relayed = lax.ppermute(z1, "ctx", inner)
    outer_near = lax.ppermute(across, "ctx", outward)
    y1 = swap(z1, 1)
    outer_far = lax.ppermute(relayed, "ctx", outward)
    z2 = after(jnp.where(inside, relayed, outer_near))
    y2 = swap(z2, 1)
    z3 = after(jnp.where(inside, across, outer_far))
    y3 = swap(z3, 1)
    return [own, y0, z1, y1, z2, y2, z3, y3]


def scatter_ctx(blocks):
    other = [swap(blocks[2 * dz + 1], 1) for dz in range(4)]
    far3 = (blocks[6].astype(F32) + other[3].astype(F32)).astype(BF16)
    via = swap(far3, 2)
    far2 = (blocks[4].astype(F32) + other[2].astype(F32) + via.astype(F32)).astype(BF16)
    across = swap(far2, 4)
    near = (blocks[2].astype(F32) + after(other[1], far2).astype(F32)).astype(BF16)
    beside = swap(near, 2)
    return blocks[0].astype(F32) + other[0].astype(F32) + across.astype(F32) + beside.astype(F32)


def gather_small(v, flat):
    blocks = v
    for b in (2, 1, 0, 3, 4):
        other = hop(blocks, 1 << b)
        high = ((flat >> b) & 1) == 1
        blocks = jnp.where(high, jnp.stack([other, blocks]), jnp.stack([blocks, other]))
    return blocks.transpose((0, 1, 4, 3, 2, 5, 6)).reshape((32,) + v.shape)


def sum_small(v):
    for b in (2, 1, 3, 4, 0):
        v = v + hop(v, 1 << b)
    return v


def dot(left, right, dims):
    return lax.dot_general(left, right, (dims, ((), ())), preferred_element_type=F32)


def full(shape, **kw):
    return pl.BlockSpec(shape, lambda *_: (0,) * len(shape), **kw)


def call(kernel, *rest, **kw):
    inner = kernel_call(kernel, *rest, **kw)

    return inner


def kernel_call(kernel, grid, in_specs, out_specs, out_shape, flops, moved, exps=0, scratch=()):
    return pl.pallas_call(
        kernel,
        grid_spec=pltpu.PrefetchScalarGridSpec(
            num_scalar_prefetch=1,
            grid=grid,
            in_specs=in_specs,
            out_specs=out_specs,
            scratch_shapes=list(scratch),
        ),
        out_shape=out_shape,
        cost_estimate=pl.CostEstimate(flops=flops, bytes_accessed=moved, transcendentals=exps),
    )


def struct(shape, dtype):
    return jax.ShapeDtypeStruct(shape, dtype)


def take_pair(step, odd, chunks, block):
    half = block.shape[0] // 2
    for i in range(4):

        @pl.when(step == i)
        def _():
            block[pl.ds(pl.multiple_of(odd * half, half), half)] = chunks[2 * i][...]
            block[pl.ds(pl.multiple_of((1 - odd) * half, half), half)] = chunks[2 * i + 1][...]


def pair_at(d, c):
    return ((c[0] >> 1) ^ d, 0)


def projection_kernel(c_ref, *refs):
    chunks = refs[:8]
    packed = refs[8:12]
    wgt, g1, gq, gk, cosine, sine = refs[12:18]
    x_out, xn_out, q_out, k_out, v_out, qr_out, kr_out, gate_out, weights = refs[18:27]
    block = refs[27]
    d = pl.program_id(0)
    odd = c_ref[0] & 1

    @pl.when(d == 0)
    def _():
        for e in range(4):
            j = c_ref[1] ^ e
            for start, size, first in ((0, 64, 0), (256, 32, 64), (384, 32, 96)):
                at = pl.multiple_of(start + size * j, size)
                weights[pl.ds(at, size)] = packed[e][first : first + size]

    take_pair(d, odd, chunks, block)
    x_out[...] = block[...]
    x = block[...].astype(F32)
    xn = (x * lax.rsqrt(jnp.mean(x * x, axis=-1, keepdims=True) + EPS) * g1[...]).astype(BF16)
    xn_out[...] = xn
    made = dot(xn, weights[...], LAST)
    gate_out[...] = jax.nn.sigmoid(dot(xn, wgt[...], LAST))
    q_out[...] = made[:, :256]
    k_out[...] = made[:, 256:384]
    v_out[...] = made[:, 384:].astype(BF16)

    def turned(v, gain):
        v = v * lax.rsqrt(jnp.mean(v * v, axis=-1, keepdims=True) + EPS) * gain
        return (v * cosine[...] + pltpu.roll(v, HD // 2, 1) * sine[...]).astype(BF16)

    qr_out[:, :HD] = turned(made[:, :HD], gq[...])
    qr_out[:, HD:] = turned(made[:, HD : 2 * HD], gq[...])
    kr_out[...] = turned(made[:, 2 * HD : 3 * HD], gk[...])


def projection(c, chunks, packed, wgt, g1, gq, gk, cosine, sine):
    rows, width = chunks[0].shape
    length = 8 * rows
    at = pair_at
    return call(
        projection_kernel,
        (4,),
        [full((rows, width), pipeline_mode=pl.Buffered(1))] * 8
        + [
            *[full((128, width), pipeline_mode=pl.Buffered(1))] * 4,
            full(wgt.shape),
            full((1, width)),
            full((1, HD)),
            full((1, HD)),
            pl.BlockSpec((2 * rows, HD), at),
            pl.BlockSpec((2 * rows, HD), at),
        ],
        [
            *(pl.BlockSpec((2 * rows, n), at) for n in (width, width, 2 * HD, HD, HD, 2 * HD, HD, 16)),
            full((512, width)),
        ],
        [
            struct((length, width), BF16),
            struct((length, width), BF16),
            struct((length, 2 * HD), F32),
            struct((length, HD), F32),
            struct((length, HD), BF16),
            struct((length, 2 * HD), BF16),
            struct((length, HD), BF16),
            struct((length, 16), F32),
            struct((512, width), BF16),
        ],
        2 * length * width * 528,
        20 * length * width,
        scratch=[pltpu.VMEM((2 * rows, width), BF16)],
    )(c, *chunks, *packed, wgt, g1, gq, gk, cosine, sine)


def head_column(ref):
    value = ref[...]
    return jnp.where(pl.program_id(0) == 0, value[:, 0:1], value[:, 1:2])


def attention_kernel(
    c_ref, limit_ref, pos_ref, q_ref, k_ref, v_ref, gate_ref, out_ref, mixed_ref, lse_ref
):
    scores = dot(q_ref[...], k_ref[...], LAST) * (HD**-0.5)
    scores = jnp.where(pos_ref[...] <= limit_ref[...], scores, NEG)
    top = jnp.max(scores, axis=-1, keepdims=True)
    weights = jnp.exp(scores - top)
    total = jnp.sum(weights, axis=-1, keepdims=True)
    probs = (weights * (1.0 / total)).astype(BF16)
    attended = jnp.dot(probs, v_ref[...], preferred_element_type=F32)
    out_ref[...] = attended
    mixed_ref[...] = (attended * head_column(gate_ref)).astype(BF16)
    lse_ref[0] = top + jnp.log(total)


def attention(c, q, k, v, gates, limit, pos, tile=256):
    length = q.shape[0]
    return call(
        attention_kernel,
        (2, length // tile),
        [
            pl.BlockSpec((tile, 1), lambda h, i, c: (i, 0)),
            full((1, length)),
            pl.BlockSpec((tile, HD), lambda h, i, c: (i, h)),
            full((length, HD)),
            full((length, HD)),
            pl.BlockSpec((tile, 16), lambda h, i, c: (i, 0)),
        ],
        [
            pl.BlockSpec((tile, HD), lambda h, i, c: (i, h)),
            pl.BlockSpec((tile, HD), lambda h, i, c: (i, h)),
            pl.BlockSpec((1, tile, 1), lambda h, i, c: (h, i, 0)),
        ],
        [
            struct((length, 2 * HD), F32),
            struct((length, 2 * HD), BF16),
            struct((2, length, 1), F32),
        ],
        8 * length * length * HD,
        16 * length * HD,
        2 * length * length,
    )(c, limit, pos, q, k, v, gates)


def hidden_kernel(c_ref, *refs):
    mixed = refs[:8]
    x, wo, g2 = refs[8:11]
    xn_out, own_out = refs[11:13]
    left, total = refs[13:]
    c = c_ref[0]
    odd = c & 1
    for d in range(8):
        other = c ^ d
        at = pl.multiple_of(256 * (2 * (other & 3) + (other >> 2)), 256)
        left[:, pl.ds(at, 256)] = mixed[d][...]
    for n in range(0, total.shape[1], 512):
        cols = slice(n, n + 512)
        total[:, cols] = x[:, cols].astype(F32) + jnp.dot(
            left[...], wo[:, cols], preferred_element_type=F32
        )
    h = total[...]
    xn = (h * lax.rsqrt(jnp.mean(h * h, axis=-1, keepdims=True) + EPS) * g2[...]).astype(BF16)
    xn_out[pl.ds(pl.multiple_of(odd * 128, 128), 128)] = xn[:128]
    xn_out[pl.ds(pl.multiple_of((1 - odd) * 128, 128), 128)] = xn[128:]

    @pl.when(pl.program_id(0) == c >> 1)
    def _():
        own_out[...] = total[pl.ds(pl.multiple_of(odd * 128, 128), 128)]


def hidden(c, mixed, x_all, wo, g2):
    length, width = x_all.shape
    return call(
        hidden_kernel,
        (4,),
        [pl.BlockSpec((256, 256), lambda i, c: (i, 0))] * 8
        + [
            pl.BlockSpec((256, width), lambda i, c: (i, 0)),
            full((width, width), pipeline_mode=pl.Buffered(1)),
            full((1, width)),
        ],
        [pl.BlockSpec((256, width), pair_at), full((128, width))],
        [struct((length, width), BF16), struct((128, width), F32)],
        2 * length * width * width,
        12 * length * width,
        scratch=[pltpu.VMEM((256, width), BF16), pltpu.VMEM((256, width), F32)],
    )(c, *mixed, x_all, wo, g2)


def mixed_back_kernel(c_ref, *refs):
    chunks = refs[:8]
    wo, attended, gate_ref = refs[8:11]
    all_out, att_out, logit_out = refs[11:]
    take_pair(pl.program_id(0), c_ref[0] & 1, chunks, all_out)
    grad = dot(all_out[...], wo[0], LAST)
    gates = gate_ref[...]
    lane = lax.broadcasted_iota(jnp.int32, gates.shape, 1)
    logits = jnp.zeros_like(gates)
    for h in range(2):
        part = grad[:, h * HD : (h + 1) * HD]
        gate = gates[:, h : h + 1]
        att_out[:, h * HD : (h + 1) * HD] = (part * gate).astype(BF16)
        along = jnp.sum(part * attended[:, h * HD : (h + 1) * HD], axis=-1, keepdims=True)
        logits = jnp.where(lane == h, along * gate * (1.0 - gate), logits)
    logit_out[...] = logits.astype(BF16)


def mixed_back(c, chunks, wo, attended, gates):
    rows, width = chunks[0].shape
    length = 8 * rows
    at = pair_at
    return call(
        mixed_back_kernel,
        (4,),
        [full((rows, width), pipeline_mode=pl.Buffered(1))] * 8
        + [
            pl.BlockSpec((1, 256, width), lambda d, c: (2 * (c[0] & 3) + (c[0] >> 2), 0, 0)),
            pl.BlockSpec((2 * rows, 256), at),
            pl.BlockSpec((2 * rows, 16), at),
        ],
        [pl.BlockSpec((2 * rows, n), at) for n in (width, 256, 16)],
        [struct((length, n), BF16) for n in (width, 256, 16)],
        512 * length * width,
        6 * length * width,
    )(c, *chunks, wo.reshape(8, 256, width), attended, gates)


def attention_back_kernel(c_ref, *refs):
    limit_ref, pos_ref, qr, kr, v, lse_ref, g, q_pre, k_pre, cosine, sine, cosine_all, sine_all = refs[:13]
    gq, gk = refs[13:15]
    gq_out, gk_out, gv_out, gains_out = refs[15:19]
    gk_sum, gv_sum = refs[19:]
    first = (pl.program_id(0) == 0) & (pl.program_id(1) == 0)
    last = (pl.program_id(0) == 1) & (pl.program_id(1) == pl.num_programs(1) - 1)

    def back(rotated, pre, gain, cos_ref, sin_ref):
        grad = rotated.astype(BF16).astype(F32)
        grad = grad * cos_ref[...] - pltpu.roll(grad, HD // 2, 1) * sin_ref[...]
        scale = lax.rsqrt(jnp.mean(pre * pre, axis=-1, keepdims=True) + EPS)
        weighted = grad * gain
        out = scale * weighted - pre * (scale * scale * scale) * jnp.mean(
            weighted * pre, axis=-1, keepdims=True
        )
        return out.astype(BF16), jnp.sum(grad * pre * scale, axis=0, keepdims=True)

    @pl.when(first)
    def _():
        gk_sum[...] = jnp.zeros_like(gk_sum)
        gv_sum[...] = jnp.zeros_like(gv_sum)
        gains_out[...] = jnp.zeros_like(gains_out)

    scores = dot(qr[...], kr[...], LAST) * (HD**-0.5)
    scores = jnp.where(pos_ref[...] <= limit_ref[...], scores, NEG)
    probs = jnp.exp(scores - lse_ref[0])
    grad_probs = dot(g[...], v[...], LAST)
    delta = jnp.sum(probs * grad_probs, axis=-1, keepdims=True)
    grad_scores = (probs * (grad_probs - delta)).astype(BF16)
    rotated = jnp.dot(grad_scores, kr[...], preferred_element_type=F32) * (HD**-0.5)
    gk_sum[...] += dot(grad_scores, qr[...], ROWS)
    gv_sum[...] += dot(probs.astype(BF16), g[...], ROWS)
    gq_out[...], terms = back(rotated, q_pre[...], gq[...], cosine, sine)
    gains_out[0:1] += terms

    @pl.when(last)
    def _():
        gk_out[...], key_terms = back(
            gk_sum[...] * (HD**-0.5), k_pre[...], gk[...], cosine_all, sine_all
        )
        gains_out[1:2] += key_terms
        gv_out[...] = gv_sum[...].astype(BF16)


def attention_back(c, qr, kr, v, lse, grad, q_pre, k_pre, cosine, sine, gq, gk, limit, pos, tile=256):
    length = qr.shape[0]
    mine = pl.BlockSpec((tile, HD), lambda h, i, c: (i, h))
    rows = pl.BlockSpec((tile, HD), lambda h, i, c: (i, 0))
    whole = full((length, HD))
    return call(
        attention_back_kernel,
        (2, length // tile),
        [
            pl.BlockSpec((tile, 1), lambda h, i, c: (i, 0)),
            full((1, length)),
            mine,
            whole,
            whole,
            pl.BlockSpec((1, tile, 1), lambda h, i, c: (h, i, 0)),
            mine,
            mine,
            whole,
            rows,
            rows,
            whole,
            whole,
            full((1, HD)),
            full((1, HD)),
        ],
        [mine, whole, whole, full((8, HD))],
        [
            struct((length, 2 * HD), BF16),
            struct((length, HD), BF16),
            struct((length, HD), BF16),
            struct((8, HD), F32),
        ],
        20 * length * length * HD,
        40 * length * HD,
        2 * length * length,
        scratch=[pltpu.VMEM((length, HD), F32), pltpu.VMEM((length, HD), F32)],
    )(c, limit, pos, qr, kr, v, lse, grad, q_pre, k_pre, cosine, sine, cosine, sine, gq, gk)


def input_back_kernel(c_ref, *refs):
    gq, gk, gv, logits, weights, wgt, xn, g1, start = refs[:9]
    outs = refs[9:13]
    bundle, gate_sum, held = refs[13:]
    d = pl.program_id(0)
    mine = 2 * (c_ref[0] & 3) + (c_ref[0] >> 2)

    @pl.when(d == 0)
    def _():
        bundle[...] = start[...]
        bundle[16:17] = start[16:17] * g1[...]
        gate_sum[...] = jnp.zeros_like(gate_sum)

    part = jnp.dot(gq[...], weights[:256], preferred_element_type=F32)
    part += jnp.dot(
        jnp.concatenate([gk[...], gv[...]], axis=1), weights[256:], preferred_element_type=F32
    )
    part += jnp.dot(logits[...], wgt[...], preferred_element_type=F32)
    bundle[16:17] += jnp.sum(part * xn[...].astype(F32), axis=0, keepdims=True)
    gate_sum[...] += dot(logits[...], xn[...], ROWS)
    held[...] = part.astype(BF16)
    odd = c_ref[0] & 1
    for i in range(2):

        @pl.when(d == i)
        def _():
            outs[2 * i][...] = held[pl.ds(pl.multiple_of(odd * 128, 128), 128)]
            outs[2 * i + 1][...] = held[pl.ds(pl.multiple_of((1 - odd) * 128, 128), 128)]

    @pl.when(d == 1)
    def _():
        bundle[16:17] = bundle[16:17] / g1[...]
        for g in range(8):

            @pl.when(mine == g)
            def _():
                bundle[2 * g : 2 * g + 2] += gate_sum[0:2]


def input_back(c, base, gq, gk, gv, logits, weights, wgt, xn, g1, start):
    length, width = xn.shape
    rows = length // 8
    at = lambda d, c: ((c[0] >> 1) ^ (d + base), 0)
    return call(
        input_back_kernel,
        (2,),
        [pl.BlockSpec((2 * rows, n), at) for n in (256, HD, HD, 16)]
        + [
            full(weights.shape, pipeline_mode=pl.Buffered(1)),
            full(wgt.shape),
            pl.BlockSpec((2 * rows, width), at),
            full((1, width)),
            full((24, width)),
        ],
        [full((rows, width))] * 4 + [full((24, width))],
        [struct((rows, width), BF16)] * 4 + [struct((24, width), F32)],
        528 * length * width,
        4 * length * width,
        scratch=[pltpu.VMEM((16, width), F32), pltpu.VMEM((2 * rows, width), BF16)],
    )(c, gq, gk, gv, logits, weights, wgt, xn, g1, start)


def per_device_small(*args):
    return layer_small(*args)


def layer_small(
    tokens,
    prefix,
    span_order,
    w_query,
    w_key,
    w_value,
    w_out,
    w_headgate,
    attn_gain,
    query_gain,
    key_gain,
    mlp_gain,
    w_gate,
    w_up,
    w_down,
    cotangent,
):
    rows, width = tokens.shape
    length = 8 * rows
    span = rows // 2
    s = lax.axis_index("seq")
    c = lax.axis_index("ctx")
    flat = 8 * s + c
    mine = 2 * (c & 3) + (c >> 2)
    cs = jnp.stack([c, s]).astype(jnp.int32)

    small = jnp.concatenate(
        [
            w_headgate,
            attn_gain[None],
            mlp_gain[None],
            jnp.pad(jnp.concatenate([query_gain, key_gain]), (0, 56))[None],
            jnp.zeros((13, 64), BF16),
        ],
        axis=0,
    )
    smalls = gather_small(small, flat)
    wgt = smalls[:, :16].transpose(1, 0, 2).reshape(H, width)
    wgt = lax.dynamic_slice_in_dim(jnp.concatenate([wgt, wgt], 0), 2 * mine, 16, 0)
    g1 = smalls[:, 16].reshape(1, width).astype(F32)
    g2 = smalls[:, 17].reshape(1, width).astype(F32)
    gq = smalls[:, 18, :4].reshape(1, HD).astype(F32)
    gk = smalls[:, 18, 4:8].reshape(1, HD).astype(F32)

    x_chunks = gather_ctx(tokens)
    local = jnp.concatenate([w_query, w_key, w_value], axis=0)
    packed = [turn(local)]
    packed.append(hop(packed[0], 8))
    packed.append(hop(packed[0], 16))
    packed.append(hop(packed[2], 8))
    ff = lax.all_gather(jnp.concatenate([w_gate, w_up, w_down], axis=0), "seq", axis=0)
    wg, wu, wd = (v.reshape(768, width) for v in jnp.split(ff, 3, axis=1))
    wo = lax.all_gather(w_out, BOTH, axis=0, tiled=True)

    pos = (span_order[0][:, None] * span + jnp.arange(span, dtype=jnp.int32)).reshape(length)
    limit = jnp.maximum(pos, prefix[0] - 1)
    half = HD // 2
    inv_freq = 1.0 / ROPE_BASE ** (jnp.arange(half, dtype=F32) * 2.0 / HD)
    angles = pos.astype(F32)[:, None] * inv_freq[None, :]
    cosine = jnp.cos(angles)
    sine = jnp.sin(angles)
    cosine = jnp.concatenate([cosine, cosine], axis=1)
    sine = jnp.concatenate([-sine, sine], axis=1)
    limit = limit[:, None]
    pos = pos[None, :]

    x_all, xn1, q_pre, k_pre, value, qr, kr, gates, w_qkv = projection(
        cs, x_chunks, packed, wgt, g1, gq, gk, cosine, sine
    )
    cot_chunks = gather_ctx(cotangent)
    attended, mixed, lse = attention(cs, qr, kr, value, gates, limit, pos)
    mixed_chunks = gather_ctx(mixed)
    xn2_all, hidden1 = hidden(cs, mixed_chunks, x_all, wo, g2)
    cot_all = jnp.concatenate(cot_chunks, axis=0)

    gate = project(xn2_all, wg)
    up = project(xn2_all, wu)
    grad_act = project(cot_all, wd)
    sig = jax.nn.sigmoid(gate)
    silu = gate * sig
    act = (silu * up).astype(BF16)
    grad_gate = (grad_act * up * sig * (1.0 + gate * (1.0 - sig))).astype(BF16)
    grad_up = (grad_act * silu).astype(BF16)

    grad_xn2_part = (
        jnp.dot(grad_gate, wg, preferred_element_type=F32)
        + jnp.dot(grad_up, wu, preferred_element_type=F32)
    ).astype(BF16)
    grad_xn2 = scatter_ctx(jnp.split(grad_xn2_part, 8, axis=0))
    ff_grads = []
    for left, right in ((grad_gate, xn2_all), (grad_up, xn2_all), (act, cot_all)):
        ff_grads.append(outer(left, right).astype(BF16))
    joined = jnp.concatenate([v.reshape(4, 192, width) for v in ff_grads], axis=1)
    summed = lax.psum_scatter(joined.reshape(2304, width), "seq", scatter_dimension=0, tiled=True)
    grad_w_gate, grad_w_up, grad_w_down = jnp.split(summed.astype(F32), 3, axis=0)
    branch_part = jnp.dot(act, wd, preferred_element_type=F32).astype(BF16)

    _, scale2 = norm_apply(hidden1, g2)
    grad_h1_norm, gain2_terms = norm_back(hidden1, scale2, g2, grad_xn2)
    grad_hidden1 = cotangent.astype(F32) + grad_h1_norm
    grad_gain2 = jnp.sum(gain2_terms, axis=0)
    branch_chunks = gather_ctx(after(grad_hidden1.astype(BF16), *ff_grads, branch_part))
    grad_branch_all, grad_att, grad_logits = mixed_back(cs, branch_chunks, wo, attended, gates)
    grad_wo = outer(mixed, grad_branch_all).astype(BF16)
    branch_part = after(branch_part, *branch_chunks)
    branch = scatter_ctx(jnp.split(branch_part, 8, axis=0))
    output = (hidden1 + branch).astype(BF16)

    gq_rows, gk_rows, gv_rows, head_gains = attention_back(
        cs, qr, kr, value, lse, grad_att, q_pre, k_pre, cosine, sine, gq, gk, limit, pos
    )
    heads = jnp.pad(head_gains[:2].reshape(1, 2 * HD), ((0, 0), (0, width - 2 * HD)))
    bundle = jnp.concatenate(
        [jnp.zeros((17, width), F32), grad_gain2[None], heads, jnp.zeros((5, width), F32)], axis=0
    )
    shared = (gq_rows, gk_rows, gv_rows, grad_logits, w_qkv, wgt, xn1, g1)
    *far, bundle = input_back(cs, 2, *shared, bundle)
    *close, bundle = input_back(cs, 0, *shared, bundle)
    grad_xn1 = scatter_ctx(close + far)
    x = tokens.astype(F32)
    scale1 = lax.rsqrt(jnp.mean(x * x, axis=-1, keepdims=True) + EPS)
    grad_x, _ = norm_back(x, scale1, g1, grad_xn1)
    grad_tokens = grad_hidden1 + grad_x

    g_wo = lax.psum_scatter(grad_wo, "seq", scatter_dimension=0, tiled=True)
    g_wo = turn(g_wo).astype(F32)
    pieces = jnp.concatenate(
        [
            outer(gq_rows, xn1).astype(BF16).reshape(2, 2, 64, width),
            outer(gk_rows, xn1).astype(BF16).reshape(2, 2, 32, width),
            outer(gv_rows, xn1).astype(BF16).reshape(2, 2, 32, width),
        ],
        axis=2,
    )
    for axis, bit in ((1, s & 1), (0, s >> 1)):
        sent = lax.dynamic_index_in_dim(pieces, 1 - bit, axis, keepdims=False)
        kept = lax.dynamic_index_in_dim(pieces, bit, axis, keepdims=False)
        got = hop(sent, 8 if axis else 16)
        pieces = (kept.astype(F32) + got.astype(F32)).astype(BF16)
    home = turn(pieces)
    g_wq, g_wk, g_wv = (v.astype(F32) for v in jnp.split(home, (64, 96), axis=0))

    bundle = sum_small(bundle)
    blocks = lax.dynamic_slice_in_dim(bundle[:18], 64 * flat, 64, 1)
    heads = lax.dynamic_slice_in_dim(bundle[18, : 2 * HD].reshape(2, HD), 4 * flat, 4, 1)
    return (
        output,
        grad_tokens,
        g_wq,
        g_wk,
        g_wv,
        g_wo,
        blocks[:16],
        blocks[16],
        heads[0],
        heads[1],
        blocks[17],
        grad_w_gate,
        grad_w_up,
        grad_w_down,
    )


def solution(mesh):
    in_specs = (
        P(("seq", "ctx"), None),
        P("seq"),
        P("seq", None),
        P(("seq", "ctx"), None),
        P(("seq", "ctx"), None),
        P(("seq", "ctx"), None),
        P(("seq", "ctx"), None),
        P(None, ("seq", "ctx")),
        P(("seq", "ctx")),
        P(("seq", "ctx")),
        P(("seq", "ctx")),
        P(("seq", "ctx")),
        P(("seq", "ctx"), None),
        P(("seq", "ctx"), None),
        P(("seq", "ctx"), None),
        P(("seq", "ctx"), None),
    )
    out_specs = (
        P(("seq", "ctx"), None),
        P(("seq", "ctx"), None),
        P(("seq", "ctx"), None),
        P(("seq", "ctx"), None),
        P(("seq", "ctx"), None),
        P(("seq", "ctx"), None),
        P(None, ("seq", "ctx")),
        P(("seq", "ctx")),
        P(("seq", "ctx")),
        P(("seq", "ctx")),
        P(("seq", "ctx")),
        P(("seq", "ctx"), None),
        P(("seq", "ctx"), None),
        P(("seq", "ctx"), None),
    )
    sizes = dict(mesh.shape)
    small = sizes == {"seq": 4, "ctx": 8}
    return jax.shard_map(
        per_device_small if small else per_device, mesh=mesh, in_specs=in_specs, out_specs=out_specs, check_vma=False
    )
```

```python
import jax
import jax.numpy as jnp
from jax import lax
from jax.experimental import pallas as pl
from jax.experimental.pallas import tpu as pltpu

from jax.sharding import PartitionSpec as P

H = 16
KVH = 8
HD = 128


EPS = 1e-06
ROPE_BASE = 1000000.0
NEG = -1e30


def rotate(v, positions, sign):
    half = v.shape[-1] // 2
    inv_freq = 1.0 / ROPE_BASE ** (jnp.arange(half, dtype=jnp.float32) * 2.0 / v.shape[-1])
    angles = positions.astype(jnp.float32)[:, None] * inv_freq[None, :]
    cosine = jnp.cos(angles)[:, None, :]
    sine = sign * jnp.sin(angles)[:, None, :]
    first = v[..., :half]
    second = v[..., half:]
    return jnp.concatenate(
        [first * cosine - second * sine, second * cosine + first * sine], axis=-1
    )


def norm_apply(v, gain):
    factor = lax.rsqrt(jnp.mean(v * v, axis=-1, keepdims=True) + EPS)
    return (v * factor * gain, factor)


def norm_back(v, factor, gain, grad):
    weighted = grad * gain
    grad_v = factor * weighted - v * (factor * factor * factor) * jnp.mean(
        weighted * v, axis=-1, keepdims=True
    )
    return (grad_v, grad * v * factor)


def project(left, right):
    return lax.dot_general(
        left, right, (((1,), (1,)), ((), ())), preferred_element_type=jnp.float32
    )


def outer(left, right):
    return lax.dot_general(
        left, right, (((0,), (0,)), ((), ())), preferred_element_type=jnp.float32
    )


def block_scores(query_block, key_block, allowed, factor):
    scores = (
        jnp.einsum("hgtd,khd->hgtk", query_block, key_block, preferred_element_type=jnp.float32)
        * factor
    )
    return jnp.where(allowed[None, None], scores, NEG)


def per_device(
    tokens,
    prefix,
    span_order,
    w_query,
    w_key,
    w_value,
    w_out,
    w_headgate,
    attn_gain,
    query_gain,
    key_gain,
    mlp_gain,
    w_gate,
    w_up,
    w_down,
    cotangent,
):
    rows = tokens.shape[0]
    span = rows // 2
    length = rows * lax.axis_size("ctx")
    heads = H
    kv_heads = KVH
    head = HD
    group = heads // kv_heads
    pair = 2
    pairs = kv_heads // pair
    factor = head ** (-0.5)
    order = span_order[0]
    offsets = jnp.arange(span, dtype=jnp.int32)
    every_pos = (order[:, None] * span + offsets[None, :]).reshape(length)
    mine = lax.dynamic_slice_in_dim(every_pos, lax.axis_index("ctx") * rows, rows)
    limit = jnp.maximum(mine, prefix[0] - 1)
    allowed = every_pos[None, :] <= limit[:, None]
    wq, wk, wv, wo, wgt, g1, gq, gk, g2 = (
        lax.all_gather(w_query, ("seq", "ctx"), axis=0, tiled=True),
        lax.all_gather(w_key, ("seq", "ctx"), axis=0, tiled=True),
        lax.all_gather(w_value, ("seq", "ctx"), axis=0, tiled=True),
        lax.all_gather(w_out, ("seq", "ctx"), axis=0, tiled=True),
        lax.all_gather(w_headgate, ("seq", "ctx"), axis=1, tiled=True),
        lax.all_gather(attn_gain, ("seq", "ctx"), axis=0, tiled=True),
        lax.all_gather(query_gain, ("seq", "ctx"), axis=0, tiled=True),
        lax.all_gather(key_gain, ("seq", "ctx"), axis=0, tiled=True),
        lax.all_gather(mlp_gain, ("seq", "ctx"), axis=0, tiled=True),
    )
    x = tokens.astype(jnp.float32)
    xn1_full, scale1 = norm_apply(x, g1.astype(jnp.float32))
    xn1 = xn1_full.astype(jnp.bfloat16)
    query = project(xn1, wq).reshape(rows, heads, head)
    key = project(xn1, wk).reshape(rows, kv_heads, head)
    value = project(xn1, wv).astype(jnp.bfloat16)
    logits = project(xn1, wgt)
    query_normed, query_scale = norm_apply(query, gq.astype(jnp.float32))
    key_normed, key_scale = norm_apply(key, gk.astype(jnp.float32))
    query_rot = rotate(query_normed, mine, 1.0).astype(jnp.bfloat16)
    key_rot = rotate(key_normed, mine, 1.0).astype(jnp.bfloat16).reshape(rows, kv_heads * head)
    keys_all, values_all = (
        lax.all_gather(key_rot, "ctx", axis=0, tiled=True),
        lax.all_gather(value, "ctx", axis=0, tiled=True),
    )
    query_blocks = query_rot.reshape(rows, pairs, pair, group, head).transpose(1, 2, 3, 0, 4)

    def forward_block(index):
        key_block = lax.dynamic_slice_in_dim(keys_all, index * pair * head, pair * head, 1).reshape(
            length, pair, head
        )
        value_block = lax.dynamic_slice_in_dim(
            values_all, index * pair * head, pair * head, 1
        ).reshape(length, pair, head)
        scores = block_scores(query_blocks[index], key_block, allowed, factor)
        lse = jax.nn.logsumexp(scores, axis=-1, keepdims=True)
        probs = jnp.exp(scores - lse).astype(jnp.bfloat16)
        return (
            jnp.einsum("hgtk,khd->hgtd", probs, value_block, preferred_element_type=jnp.float32),
            lse,
        )

    attended_blocks, lse_blocks = lax.map(forward_block, jnp.arange(pairs))
    attended = attended_blocks.transpose(3, 0, 1, 2, 4).reshape(rows, heads, head)
    gates = jax.nn.sigmoid(logits)
    mixed = (attended * gates[:, :, None]).reshape(rows, heads * head).astype(jnp.bfloat16)
    hidden1 = x + jnp.dot(mixed, wo, preferred_element_type=jnp.float32)
    xn2_full, scale2 = norm_apply(hidden1, g2.astype(jnp.float32))
    xn2 = xn2_full.astype(jnp.bfloat16)
    gate_local, up_local, down_local = (
        lax.all_gather(w_gate, "seq", axis=0, tiled=True),
        lax.all_gather(w_up, "seq", axis=0, tiled=True),
        lax.all_gather(w_down, "seq", axis=0, tiled=True),
    )
    xn2_all, grad_y_all = (
        lax.all_gather(xn2, "ctx", axis=0, tiled=True),
        lax.all_gather(cotangent, "ctx", axis=0, tiled=True),
    )
    gate_part = project(xn2_all, gate_local)
    up_part = project(xn2_all, up_local)
    act_part = (jax.nn.silu(gate_part) * up_part).astype(jnp.bfloat16)
    branch = lax.psum_scatter(
        jnp.dot(act_part, down_local, preferred_element_type=jnp.float32).astype(jnp.bfloat16),
        "ctx",
        scatter_dimension=0,
        tiled=True,
    ).astype(jnp.float32)
    output = (hidden1 + branch).astype(jnp.bfloat16)
    gate_all = project(xn2_all, gate_local)
    up_all = project(xn2_all, up_local)
    sig_all = jax.nn.sigmoid(gate_all)
    silu_all = gate_all * sig_all
    act_local = (silu_all * up_all).astype(jnp.bfloat16)
    grad_act_all = project(grad_y_all, down_local)
    grad_gate_local = (grad_act_all * up_all * sig_all * (1.0 + gate_all * (1.0 - sig_all))).astype(
        jnp.bfloat16
    )
    grad_up_local = (grad_act_all * silu_all).astype(jnp.bfloat16)
    grad_xn2 = lax.psum_scatter(
        (
            jnp.dot(grad_gate_local, gate_local, preferred_element_type=jnp.float32)
            + jnp.dot(grad_up_local, up_local, preferred_element_type=jnp.float32)
        ).astype(jnp.bfloat16),
        "ctx",
        scatter_dimension=0,
        tiled=True,
    ).astype(jnp.float32)
    grad_w_gate, grad_w_up, grad_w_down = (
        lax.psum_scatter(
            outer(grad_gate_local, xn2_all).astype(jnp.bfloat16),
            "seq",
            scatter_dimension=0,
            tiled=True,
        ).astype(jnp.float32),
        lax.psum_scatter(
            outer(grad_up_local, xn2_all).astype(jnp.bfloat16),
            "seq",
            scatter_dimension=0,
            tiled=True,
        ).astype(jnp.float32),
        lax.psum_scatter(
            outer(act_local, grad_y_all).astype(jnp.bfloat16),
            "seq",
            scatter_dimension=0,
            tiled=True,
        ).astype(jnp.float32),
    )
    grad_h1_norm, gain2_terms = norm_back(hidden1, scale2, g2.astype(jnp.float32), grad_xn2)
    grad_hidden1 = cotangent.astype(jnp.float32) + grad_h1_norm
    grad_gain2 = jnp.sum(gain2_terms, axis=0)
    grad_branch = grad_hidden1.astype(jnp.bfloat16)
    grad_w_out = outer(mixed, grad_branch)
    grad_mixed = project(grad_branch, wo).reshape(rows, heads, head)
    grad_att = (grad_mixed * gates[:, :, None]).astype(jnp.bfloat16)
    grad_logits = (jnp.sum(grad_mixed * attended, axis=-1) * gates * (1.0 - gates)).astype(
        jnp.bfloat16
    )
    grad_blocks = grad_att.reshape(rows, pairs, pair, group, head).transpose(1, 2, 3, 0, 4)

    def backward_block(index):
        key_block = lax.dynamic_slice_in_dim(keys_all, index * pair * head, pair * head, 1).reshape(
            length, pair, head
        )
        value_block = lax.dynamic_slice_in_dim(
            values_all, index * pair * head, pair * head, 1
        ).reshape(length, pair, head)
        query_block = query_blocks[index]
        grad_out = grad_blocks[index]
        scores = block_scores(query_block, key_block, allowed, factor)
        probs = jnp.exp(scores - lse_blocks[index])
        grad_probs = jnp.einsum(
            "hgtd,khd->hgtk", grad_out, value_block, preferred_element_type=jnp.float32
        )
        delta = jnp.sum(probs * grad_probs, axis=-1, keepdims=True)
        grad_scores = (probs * (grad_probs - delta)).astype(jnp.bfloat16)
        grad_query = (
            jnp.einsum("hgtk,khd->hgtd", grad_scores, key_block, preferred_element_type=jnp.float32)
            * factor
        )
        grad_key = (
            jnp.einsum(
                "hgtk,hgtd->khd", grad_scores, query_block, preferred_element_type=jnp.float32
            )
            * factor
        )
        grad_value = jnp.einsum(
            "hgtk,hgtd->khd",
            probs.astype(jnp.bfloat16),
            grad_out,
            preferred_element_type=jnp.float32,
        )
        return (grad_query, grad_key, grad_value)

    grad_query_blocks, grad_key_all, grad_value_all = lax.map(backward_block, jnp.arange(pairs))
    grad_key_sum, grad_value_sum = (
        lax.psum_scatter(
            grad_key_all.astype(jnp.bfloat16), "ctx", scatter_dimension=1, tiled=True
        ).astype(jnp.float32),
        lax.psum_scatter(
            grad_value_all.astype(jnp.bfloat16), "ctx", scatter_dimension=1, tiled=True
        ).astype(jnp.float32),
    )
    grad_value_rows = (
        grad_value_sum.astype(jnp.bfloat16).transpose(1, 0, 2, 3).reshape(rows, kv_heads * head)
    )
    grad_key_rot = (
        grad_key_sum.astype(jnp.bfloat16)
        .astype(jnp.float32)
        .transpose(1, 0, 2, 3)
        .reshape(rows, kv_heads, head)
    )
    grad_key_normed = rotate(grad_key_rot, mine, -1.0)
    grad_key_pre, key_gain_terms = norm_back(
        key, key_scale, gk.astype(jnp.float32), grad_key_normed
    )
    grad_key_rows = grad_key_pre.astype(jnp.bfloat16).reshape(rows, kv_heads * head)
    grad_key_gain = jnp.sum(key_gain_terms, axis=(0, 1))
    grad_query_rot = (
        grad_query_blocks.transpose(3, 0, 1, 2, 4)
        .reshape(rows, heads, head)
        .astype(jnp.bfloat16)
        .astype(jnp.float32)
    )
    grad_query_normed = rotate(grad_query_rot, mine, -1.0)
    grad_query_pre, query_gain_terms = norm_back(
        query, query_scale, gq.astype(jnp.float32), grad_query_normed
    )
    grad_query_rows = grad_query_pre.astype(jnp.bfloat16).reshape(rows, heads * head)
    grad_query_gain = jnp.sum(query_gain_terms, axis=(0, 1))
    grad_w_query = outer(grad_query_rows, xn1)
    grad_w_key = outer(grad_key_rows, xn1)
    grad_w_value = outer(grad_value_rows, xn1)
    grad_w_headgate = outer(grad_logits, xn1)
    grad_xn1 = jnp.dot(grad_query_rows, wq, preferred_element_type=jnp.float32) + jnp.dot(
        grad_key_rows, wk, preferred_element_type=jnp.float32
    )
    grad_xn1 = (
        grad_xn1
        + jnp.dot(grad_value_rows, wv, preferred_element_type=jnp.float32)
        + jnp.dot(grad_logits, wgt, preferred_element_type=jnp.float32)
    )
    grad_x_norm, gain1_terms = norm_back(x, scale1, g1.astype(jnp.float32), grad_xn1)
    grad_tokens = grad_hidden1 + grad_x_norm
    grad_gain1 = jnp.sum(gain1_terms, axis=0)
    summed = (
        lax.psum_scatter(grad_w_query, ("seq", "ctx"), scatter_dimension=0, tiled=True),
        lax.psum_scatter(grad_w_key, ("seq", "ctx"), scatter_dimension=0, tiled=True),
        lax.psum_scatter(grad_w_value, ("seq", "ctx"), scatter_dimension=0, tiled=True),
        lax.psum_scatter(grad_w_out, ("seq", "ctx"), scatter_dimension=0, tiled=True),
        lax.psum_scatter(grad_w_headgate, ("seq", "ctx"), scatter_dimension=1, tiled=True),
        lax.psum_scatter(grad_gain1, ("seq", "ctx"), scatter_dimension=0, tiled=True),
        lax.psum_scatter(grad_query_gain, ("seq", "ctx"), scatter_dimension=0, tiled=True),
        lax.psum_scatter(grad_key_gain, ("seq", "ctx"), scatter_dimension=0, tiled=True),
        lax.psum_scatter(grad_gain2, ("seq", "ctx"), scatter_dimension=0, tiled=True),
    )
    g_wq, g_wk, g_wv, g_wo, g_wgt, g_g1, g_gq, g_gk, g_g2 = summed
    return (
        output,
        grad_tokens,
        g_wq,
        g_wk,
        g_wv,
        g_wo,
        g_wgt,
        g_g1,
        g_gq,
        g_gk,
        g_g2,
        grad_w_gate,
        grad_w_up,
        grad_w_down,
    )


BF16 = jnp.bfloat16
F32 = jnp.float32
BOTH = ("seq", "ctx")
ROWS = ((0,), (0,))
LAST = ((1,), (1,))


def swap(v, d):
    return lax.ppermute(v, "ctx", [(c, c ^ d) for c in range(8)])


def hop(v, d):
    return lax.ppermute(v, BOTH, [(i, i ^ d) for i in range(32)])


def turn(v):
    pairs = [
        (8 * r + 4 * q + j, 8 * j + 4 * q + r) for r in range(4) for q in range(2) for j in range(4)
    ]
    return lax.ppermute(v, BOTH, pairs)


def after(v, *others):
    return lax.optimization_barrier((v, *others))[0]


def gather_ctx(own):
    inner = [(c, c ^ 6) for c in range(8) if (c >> 1) in (1, 2)]
    outward = [(c, c ^ 2) for c in range(8) if (c >> 1) in (1, 2)]
    z = lax.axis_index("ctx") >> 1
    inside = (z == 1) | (z == 2)
    z1 = swap(own, 2)
    across = lax.ppermute(own, "ctx", inner)
    y0 = swap(own, 1)
    relayed = lax.ppermute(z1, "ctx", inner)
    outer_near = lax.ppermute(across, "ctx", outward)
    y1 = swap(z1, 1)
    outer_far = lax.ppermute(relayed, "ctx", outward)
    z2 = after(jnp.where(inside, relayed, outer_near))
    y2 = swap(z2, 1)
    z3 = after(jnp.where(inside, across, outer_far))
    y3 = swap(z3, 1)
    return [own, y0, z1, y1, z2, y2, z3, y3]


def scatter_ctx(blocks):
    other = [swap(blocks[2 * dz + 1], 1) for dz in range(4)]
    far3 = (blocks[6].astype(F32) + other[3].astype(F32)).astype(BF16)
    via = swap(far3, 2)
    far2 = (blocks[4].astype(F32) + other[2].astype(F32) + via.astype(F32)).astype(BF16)
    across = swap(far2, 4)
    near = (blocks[2].astype(F32) + after(other[1], far2).astype(F32)).astype(BF16)
    beside = swap(near, 2)
    return blocks[0].astype(F32) + other[0].astype(F32) + across.astype(F32) + beside.astype(F32)


def gather_small(v, flat):
    blocks = v
    for b in (2, 1, 0, 3, 4):
        other = hop(blocks, 1 << b)
        high = ((flat >> b) & 1) == 1
        blocks = jnp.where(high, jnp.stack([other, blocks]), jnp.stack([blocks, other]))
    return blocks.transpose((0, 1, 4, 3, 2, 5, 6)).reshape((32,) + v.shape)


def sum_small(v, gate):
    for b in (3, 4, 0, 1, 2):
        got = hop(v, 1 << b)
        v = v + (after(got, gate) if b in (1, 2) else got)
    return v


def dot(left, right, dims):
    return lax.dot_general(left, right, (dims, ((), ())), preferred_element_type=F32)


def full(shape, **kw):
    return pl.BlockSpec(shape, lambda *_: (0,) * len(shape), **kw)


def call(kernel, *rest, **kw):
    inner = kernel_call(kernel, *rest, **kw)

    return inner


def kernel_call(
    kernel, grid, in_specs, out_specs, out_shape, flops, moved, exps=0, scratch=(), aliases=None
):
    return pl.pallas_call(
        kernel,
        input_output_aliases=aliases or {},
        grid_spec=pltpu.PrefetchScalarGridSpec(
            num_scalar_prefetch=1,
            grid=grid,
            in_specs=in_specs,
            out_specs=out_specs,
            scratch_shapes=list(scratch),
        ),
        out_shape=out_shape,
        cost_estimate=pl.CostEstimate(flops=flops, bytes_accessed=moved, transcendentals=exps),
    )


def struct(shape, dtype):
    return jax.ShapeDtypeStruct(shape, dtype)


def take_pair(step, odd, chunks, block):
    half = block.shape[0] // 2
    for i in range(2):

        @pl.when(step == i)
        def _():
            block[pl.ds(pl.multiple_of(odd * half, half), half)] = chunks[2 * i][...]
            block[pl.ds(pl.multiple_of((1 - odd) * half, half), half)] = chunks[2 * i + 1][...]


def pair_at(d, c):
    return ((c[0] >> 1) ^ d, 0)


def far_pair_at(d, c):
    return ((c[0] >> 1) ^ (d + 2), 0)


def anywhere(arrays):
    return [pl.BlockSpec(memory_space=pl.ANY)] * len(arrays)


def projection_kernel(c_ref, *refs):
    chunks = refs[:4]
    wgt, g1, gq, gk, cosine, sine = refs[4:10]
    first = len(refs) == 24
    if first:
        packed = refs[10:14]
        outs, weights, block = refs[14:22], refs[22], refs[23]
    else:
        weights = refs[10]
        outs, block = refs[19:27], refs[27]
    x_out, xn_out, q_out, k_out, v_out, qr_out, kr_out, gate_out = outs
    d = pl.program_id(0)

    if first:

        @pl.when(d == 0)
        def _():
            for e in range(4):
                j = c_ref[1] ^ e
                for start, size, row in ((0, 64, 0), (256, 32, 64), (384, 32, 96)):
                    at = pl.multiple_of(start + size * j, size)
                    weights[pl.ds(at, size)] = packed[e][row : row + size]

    take_pair(d, c_ref[0] & 1, chunks, block)
    x_out[...] = block[...]
    x = block[...].astype(F32)
    xn = (x * lax.rsqrt(jnp.mean(x * x, axis=-1, keepdims=True) + EPS) * g1[...]).astype(BF16)
    xn_out[...] = xn
    made = dot(xn, weights[...], LAST)
    gate_out[...] = jax.nn.sigmoid(dot(xn, wgt[...], LAST))
    q_out[...] = made[:, :256]
    k_out[...] = made[:, 256:384]
    v_out[...] = made[:, 384:].astype(BF16)

    def turned(v, gain):
        v = v * lax.rsqrt(jnp.mean(v * v, axis=-1, keepdims=True) + EPS) * gain
        return (v * cosine[...] + pltpu.roll(v, HD // 2, 1) * sine[...]).astype(BF16)

    qr_out[:, :HD] = turned(made[:, :HD], gq[...])
    qr_out[:, HD:] = turned(made[:, HD : 2 * HD], gq[...])
    kr_out[...] = turned(made[:, 2 * HD : 3 * HD], gk[...])


def projection(c, chunks, packed, wgt, g1, gq, gk, cosine, sine, before=None):
    rows, width = chunks[0].shape
    length = 8 * rows
    at = far_pair_at if before else pair_at
    given = before or packed
    weights = full((512, width), pipeline_mode=pl.Buffered(1))
    columns = ((width, BF16), (width, BF16), (256, F32), (HD, F32), (HD, BF16), (256, BF16), (HD, BF16), (16, F32))
    out_specs = [pl.BlockSpec((2 * rows, n), at) for n, _ in columns]
    out_shape = [struct((length, n), kind) for n, kind in columns]
    if before:
        given = [before[8], *before[:8]]
        given_specs = [weights, *anywhere(before[:8])]
    else:
        given_specs = [full((128, width), pipeline_mode=pl.Buffered(1))] * 4
        out_specs.append(full((512, width)))
        out_shape.append(struct((512, width), BF16))
    made = call(
        projection_kernel,
        (2,),
        [full((rows, width), pipeline_mode=pl.Buffered(1))] * 4
        + [
            full(wgt.shape),
            full((1, width)),
            full((1, HD)),
            full((1, HD)),
            pl.BlockSpec((2 * rows, HD), at),
            pl.BlockSpec((2 * rows, HD), at),
            *given_specs,
        ],
        out_specs,
        out_shape,
        length * width * 528,
        10 * length * width,
        scratch=[pltpu.VMEM((2 * rows, width), BF16)],
        aliases={12 + i: i for i in range(8)} if before else None,
    )(c, *chunks, wgt, g1, gq, gk, cosine, sine, *given)
    return [*made, before[8]] if before else made


def head_column(ref):
    value = ref[...]
    return jnp.where(pl.program_id(0) == 0, value[:, 0:1], value[:, 1:2])


def attention_kernel(
    c_ref, limit_ref, pos_ref, q_ref, k_ref, v_ref, gate_ref, out_ref, mixed_ref, lse_ref
):
    scores = dot(q_ref[...], k_ref[...], LAST) * (HD**-0.5)
    scores = jnp.where(pos_ref[...] <= limit_ref[...], scores, NEG)
    top = jnp.max(scores, axis=-1, keepdims=True)
    weights = jnp.exp(scores - top)
    total = jnp.sum(weights, axis=-1, keepdims=True)
    probs = (weights * (1.0 / total)).astype(BF16)
    attended = jnp.dot(probs, v_ref[...], preferred_element_type=F32)
    out_ref[...] = attended
    mixed_ref[...] = (attended * head_column(gate_ref)).astype(BF16)
    lse_ref[0] = top + jnp.log(total)


def attention(c, q, k, v, gates, limit, pos, tile=256):
    length = q.shape[0]
    return call(
        attention_kernel,
        (2, length // tile),
        [
            pl.BlockSpec((tile, 1), lambda h, i, c: (i, 0)),
            full((1, length)),
            pl.BlockSpec((tile, HD), lambda h, i, c: (i, h)),
            full((length, HD)),
            full((length, HD)),
            pl.BlockSpec((tile, 16), lambda h, i, c: (i, 0)),
        ],
        [
            pl.BlockSpec((tile, HD), lambda h, i, c: (i, h)),
            pl.BlockSpec((tile, HD), lambda h, i, c: (i, h)),
            pl.BlockSpec((1, tile, 1), lambda h, i, c: (h, i, 0)),
        ],
        [
            struct((length, 2 * HD), F32),
            struct((length, 2 * HD), BF16),
            struct((2, length, 1), F32),
        ],
        8 * length * length * HD,
        16 * length * HD,
        2 * length * length,
    )(c, limit, pos, q, k, v, gates)


def hidden_kernel(c_ref, *refs):
    mixed = refs[:8]
    x, wo, g2 = refs[8:11]
    xn_out, own_out = refs[11:13]
    left, total = refs[13:]
    c = c_ref[0]
    odd = c & 1
    for d in range(8):
        other = c ^ d
        at = pl.multiple_of(256 * (2 * (other & 3) + (other >> 2)), 256)
        left[:, pl.ds(at, 256)] = mixed[d][...]
    for n in range(0, total.shape[1], 512):
        cols = slice(n, n + 512)
        total[:, cols] = x[:, cols].astype(F32) + jnp.dot(
            left[...], wo[:, cols], preferred_element_type=F32
        )
    h = total[...]
    xn = (h * lax.rsqrt(jnp.mean(h * h, axis=-1, keepdims=True) + EPS) * g2[...]).astype(BF16)
    xn_out[pl.ds(pl.multiple_of(odd * 128, 128), 128)] = xn[:128]
    xn_out[pl.ds(pl.multiple_of((1 - odd) * 128, 128), 128)] = xn[128:]

    @pl.when(pl.program_id(0) == c >> 1)
    def _():
        own_out[...] = total[pl.ds(pl.multiple_of(odd * 128, 128), 128)]


def hidden(c, mixed, x_all, wo, g2):
    length, width = x_all.shape
    return call(
        hidden_kernel,
        (4,),
        [pl.BlockSpec((256, 256), lambda i, c: (i, 0))] * 8
        + [
            pl.BlockSpec((256, width), lambda i, c: (i, 0)),
            full((width, width), pipeline_mode=pl.Buffered(1)),
            full((1, width)),
        ],
        [pl.BlockSpec((256, width), pair_at), full((128, width))],
        [struct((length, width), BF16), struct((128, width), F32)],
        2 * length * width * width,
        12 * length * width,
        scratch=[pltpu.VMEM((256, width), BF16), pltpu.VMEM((256, width), F32)],
    )(c, *mixed, x_all, wo, g2)


def mixed_back_kernel(c_ref, *refs):
    chunks = refs[:4]
    wo, attended, gate_ref = refs[4:7]
    all_out, att_out, logit_out = refs[-3:]
    take_pair(pl.program_id(0), c_ref[0] & 1, chunks, all_out)
    grad = dot(all_out[...], wo[0], LAST)
    gates = gate_ref[...]
    lane = lax.broadcasted_iota(jnp.int32, gates.shape, 1)
    logits = jnp.zeros_like(gates)
    for h in range(2):
        part = grad[:, h * HD : (h + 1) * HD]
        gate = gates[:, h : h + 1]
        att_out[:, h * HD : (h + 1) * HD] = (part * gate).astype(BF16)
        along = jnp.sum(part * attended[:, h * HD : (h + 1) * HD], axis=-1, keepdims=True)
        logits = jnp.where(lane == h, along * gate * (1.0 - gate), logits)
    logit_out[...] = logits.astype(BF16)


def mixed_back(c, chunks, wo, attended, gates, before=()):
    rows, width = chunks[0].shape
    length = 8 * rows
    at = far_pair_at if before else pair_at
    return call(
        mixed_back_kernel,
        (2,),
        [full((rows, width), pipeline_mode=pl.Buffered(1))] * 4
        + [
            pl.BlockSpec((1, 256, width), lambda d, c: (2 * (c[0] & 3) + (c[0] >> 2), 0, 0)),
            pl.BlockSpec((2 * rows, 256), at),
            pl.BlockSpec((2 * rows, 16), at),
            *anywhere(before),
        ],
        [pl.BlockSpec((2 * rows, n), at) for n in (width, 256, 16)],
        [struct((length, n), BF16) for n in (width, 256, 16)],
        256 * length * width,
        3 * length * width,
        aliases={8 + i: i for i in range(3)} if before else None,
    )(c, *chunks, wo.reshape(8, 256, width), attended, gates, *before)


def attention_back_kernel(c_ref, *refs):
    limit_ref, pos_ref, qr, kr, v, lse_ref, g, q_pre, k_pre, cosine, sine, cosine_all, sine_all = refs[:13]
    gq, gk = refs[13:15]
    gq_out, gk_out, gv_out, gains_out = refs[15:19]
    gk_sum, gv_sum = refs[19:]
    first = (pl.program_id(0) == 0) & (pl.program_id(1) == 0)
    last = (pl.program_id(0) == 1) & (pl.program_id(1) == pl.num_programs(1) - 1)

    def back(rotated, pre, gain, cos_ref, sin_ref):
        grad = rotated.astype(BF16).astype(F32)
        grad = grad * cos_ref[...] - pltpu.roll(grad, HD // 2, 1) * sin_ref[...]
        scale = lax.rsqrt(jnp.mean(pre * pre, axis=-1, keepdims=True) + EPS)
        weighted = grad * gain
        out = scale * weighted - pre * (scale * scale * scale) * jnp.mean(
            weighted * pre, axis=-1, keepdims=True
        )
        return out.astype(BF16), jnp.sum(grad * pre * scale, axis=0, keepdims=True)

    @pl.when(first)
    def _():
        gk_sum[...] = jnp.zeros_like(gk_sum)
        gv_sum[...] = jnp.zeros_like(gv_sum)
        gains_out[...] = jnp.zeros_like(gains_out)

    scores = dot(qr[...], kr[...], LAST) * (HD**-0.5)
    scores = jnp.where(pos_ref[...] <= limit_ref[...], scores, NEG)
    probs = jnp.exp(scores - lse_ref[0])
    grad_probs = dot(g[...], v[...], LAST)
    delta = jnp.sum(probs * grad_probs, axis=-1, keepdims=True)
    grad_scores = (probs * (grad_probs - delta)).astype(BF16)
    rotated = jnp.dot(grad_scores, kr[...], preferred_element_type=F32) * (HD**-0.5)
    gk_sum[...] += dot(grad_scores, qr[...], ROWS)
    gv_sum[...] += dot(probs.astype(BF16), g[...], ROWS)
    gq_out[...], terms = back(rotated, q_pre[...], gq[...], cosine, sine)
    gains_out[0:1] += terms

    @pl.when(last)
    def _():
        gk_out[...], key_terms = back(
            gk_sum[...] * (HD**-0.5), k_pre[...], gk[...], cosine_all, sine_all
        )
        gains_out[1:2] += key_terms
        gv_out[...] = gv_sum[...].astype(BF16)


def attention_back(c, qr, kr, v, lse, grad, q_pre, k_pre, cosine, sine, gq, gk, limit, pos, tile=256):
    length = qr.shape[0]
    mine = pl.BlockSpec((tile, HD), lambda h, i, c: (i, h))
    rows = pl.BlockSpec((tile, HD), lambda h, i, c: (i, 0))
    whole = full((length, HD))
    return call(
        attention_back_kernel,
        (2, length // tile),
        [
            pl.BlockSpec((tile, 1), lambda h, i, c: (i, 0)),
            full((1, length)),
            mine,
            whole,
            whole,
            pl.BlockSpec((1, tile, 1), lambda h, i, c: (h, i, 0)),
            mine,
            mine,
            whole,
            rows,
            rows,
            whole,
            whole,
            full((1, HD)),
            full((1, HD)),
        ],
        [mine, whole, whole, full((8, HD))],
        [
            struct((length, 2 * HD), BF16),
            struct((length, HD), BF16),
            struct((length, HD), BF16),
            struct((8, HD), F32),
        ],
        20 * length * length * HD,
        40 * length * HD,
        2 * length * length,
        scratch=[pltpu.VMEM((length, HD), F32), pltpu.VMEM((length, HD), F32)],
    )(c, limit, pos, qr, kr, v, lse, grad, q_pre, k_pre, cosine, sine, cosine, sine, gq, gk)


def input_back_kernel(c_ref, *refs):
    gq, gk, gv, logits, weights, wgt, xn, g1, start = refs[:9]
    outs = refs[9:13]
    bundle, gate_sum, held = refs[13:]
    d = pl.program_id(0)
    mine = 2 * (c_ref[0] & 3) + (c_ref[0] >> 2)

    @pl.when(d == 0)
    def _():
        bundle[...] = start[...]
        bundle[16:17] = start[16:17] * g1[...]
        gate_sum[...] = jnp.zeros_like(gate_sum)

    part = jnp.dot(gq[...], weights[:256], preferred_element_type=F32)
    part += jnp.dot(
        jnp.concatenate([gk[...], gv[...]], axis=1), weights[256:], preferred_element_type=F32
    )
    part += jnp.dot(logits[...], wgt[...], preferred_element_type=F32)
    bundle[16:17] += jnp.sum(part * xn[...].astype(F32), axis=0, keepdims=True)
    gate_sum[...] += dot(logits[...], xn[...], ROWS)
    held[...] = part.astype(BF16)
    odd = c_ref[0] & 1
    for i in range(2):

        @pl.when(d == i)
        def _():
            outs[2 * i][...] = held[pl.ds(pl.multiple_of(odd * 128, 128), 128)]
            outs[2 * i + 1][...] = held[pl.ds(pl.multiple_of((1 - odd) * 128, 128), 128)]

    @pl.when(d == 1)
    def _():
        bundle[16:17] = bundle[16:17] / g1[...]
        for g in range(8):

            @pl.when(mine == g)
            def _():
                bundle[2 * g : 2 * g + 2] += gate_sum[0:2]


def input_back(c, base, gq, gk, gv, logits, weights, wgt, xn, g1, start):
    length, width = xn.shape
    rows = length // 8
    at = lambda d, c: ((c[0] >> 1) ^ (d + base), 0)
    return call(
        input_back_kernel,
        (2,),
        [pl.BlockSpec((2 * rows, n), at) for n in (256, HD, HD, 16)]
        + [
            full(weights.shape, pipeline_mode=pl.Buffered(1)),
            full(wgt.shape),
            pl.BlockSpec((2 * rows, width), at),
            full((1, width)),
            full((24, width)),
        ],
        [full((rows, width))] * 4 + [full((24, width))],
        [struct((rows, width), BF16)] * 4 + [struct((24, width), F32)],
        528 * length * width,
        4 * length * width,
        scratch=[pltpu.VMEM((16, width), F32), pltpu.VMEM((2 * rows, width), BF16)],
    )(c, gq, gk, gv, logits, weights, wgt, xn, g1, start)


def per_device_small(*args):
    return layer_small(*args)


def layer_small(
    tokens,
    prefix,
    span_order,
    w_query,
    w_key,
    w_value,
    w_out,
    w_headgate,
    attn_gain,
    query_gain,
    key_gain,
    mlp_gain,
    w_gate,
    w_up,
    w_down,
    cotangent,
):
    rows, width = tokens.shape
    length = 8 * rows
    span = rows // 2
    s = lax.axis_index("seq")
    c = lax.axis_index("ctx")
    flat = 8 * s + c
    mine = 2 * (c & 3) + (c >> 2)
    cs = jnp.stack([c, s]).astype(jnp.int32)

    small = jnp.concatenate(
        [
            w_headgate,
            attn_gain[None],
            mlp_gain[None],
            jnp.pad(jnp.concatenate([query_gain, key_gain]), (0, 56))[None],
            jnp.zeros((13, 64), BF16),
        ],
        axis=0,
    )
    smalls = gather_small(small, flat)
    wgt = smalls[:, :16].transpose(1, 0, 2).reshape(H, width)
    wgt = lax.dynamic_slice_in_dim(jnp.concatenate([wgt, wgt], 0), 2 * mine, 16, 0)
    g1 = smalls[:, 16].reshape(1, width).astype(F32)
    g2 = smalls[:, 17].reshape(1, width).astype(F32)
    gq = smalls[:, 18, :4].reshape(1, HD).astype(F32)
    gk = smalls[:, 18, 4:8].reshape(1, HD).astype(F32)

    x_chunks = gather_ctx(tokens)
    local = jnp.concatenate([w_query, w_key, w_value], axis=0)
    packed = [turn(local)]
    packed.append(hop(packed[0], 8))
    packed.append(hop(packed[0], 16))
    packed.append(hop(packed[2], 8))
    ff = lax.all_gather(jnp.concatenate([w_gate, w_up, w_down], axis=0), "seq", axis=0)
    wg, wu, wd = (v.reshape(768, width) for v in jnp.split(ff, 3, axis=1))
    wo = lax.all_gather(w_out, BOTH, axis=0, tiled=True)

    pos = (span_order[0][:, None] * span + jnp.arange(span, dtype=jnp.int32)).reshape(length)
    limit = jnp.maximum(pos, prefix[0] - 1)
    half = HD // 2
    inv_freq = 1.0 / ROPE_BASE ** (jnp.arange(half, dtype=F32) * 2.0 / HD)
    angles = pos.astype(F32)[:, None] * inv_freq[None, :]
    cosine = jnp.cos(angles)
    sine = jnp.sin(angles)
    cosine = jnp.concatenate([cosine, cosine], axis=1)
    sine = jnp.concatenate([-sine, sine], axis=1)
    limit = limit[:, None]
    pos = pos[None, :]

    shared = (packed, wgt, g1, gq, gk, cosine, sine)
    near = projection(cs, x_chunks[:4], *shared)
    x_all, xn1, q_pre, k_pre, value, qr, kr, gates, w_qkv = projection(
        cs, x_chunks[4:], *shared, before=near
    )
    cot_chunks = gather_ctx(cotangent)
    attended, mixed, lse = attention(cs, qr, kr, value, gates, limit, pos)
    mixed_chunks = gather_ctx(mixed)
    xn2_all, hidden1 = hidden(cs, mixed_chunks, x_all, wo, g2)
    cot_all = jnp.concatenate(cot_chunks, axis=0)

    gate = project(xn2_all, wg)
    up = project(xn2_all, wu)
    grad_act = project(cot_all, wd)
    sig = jax.nn.sigmoid(gate)
    silu = gate * sig
    act = (silu * up).astype(BF16)
    grad_gate = (grad_act * up * sig * (1.0 + gate * (1.0 - sig))).astype(BF16)
    grad_up = (grad_act * silu).astype(BF16)

    grad_xn2_part = (
        jnp.dot(grad_gate, wg, preferred_element_type=F32)
        + jnp.dot(grad_up, wu, preferred_element_type=F32)
    ).astype(BF16)
    grad_xn2 = scatter_ctx(jnp.split(grad_xn2_part, 8, axis=0))
    ff_grads = []
    for left, right in ((grad_gate, xn2_all), (grad_up, xn2_all), (act, cot_all)):
        ff_grads.append(outer(left, right).astype(BF16))
    joined = jnp.concatenate([v.reshape(4, 192, width) for v in ff_grads], axis=1)
    summed = lax.psum_scatter(joined.reshape(2304, width), "seq", scatter_dimension=0, tiled=True)
    grad_w_gate, grad_w_up, grad_w_down = jnp.split(summed.astype(F32), 3, axis=0)
    branch_part = jnp.dot(act, wd, preferred_element_type=F32).astype(BF16)

    _, scale2 = norm_apply(hidden1, g2)
    grad_h1_norm, gain2_terms = norm_back(hidden1, scale2, g2, grad_xn2)
    grad_hidden1 = cotangent.astype(F32) + grad_h1_norm
    grad_gain2 = jnp.sum(gain2_terms, axis=0)
    branch_chunks = gather_ctx(after(grad_hidden1.astype(BF16), *ff_grads, branch_part))
    near = mixed_back(cs, branch_chunks[:4], wo, attended, gates)
    grad_branch_all, grad_att, grad_logits = mixed_back(
        cs, branch_chunks[4:], wo, attended, gates, before=near
    )
    grad_wo = outer(mixed, grad_branch_all).astype(BF16)
    branch_part = after(branch_part, *branch_chunks)
    branch = scatter_ctx(jnp.split(branch_part, 8, axis=0))
    output = (hidden1 + branch).astype(BF16)

    gq_rows, gk_rows, gv_rows, head_gains = attention_back(
        cs, qr, kr, value, lse, grad_att, q_pre, k_pre, cosine, sine, gq, gk, limit, pos
    )
    heads = jnp.pad(head_gains[:2].reshape(1, 2 * HD), ((0, 0), (0, width - 2 * HD)))
    bundle = jnp.concatenate(
        [jnp.zeros((17, width), F32), grad_gain2[None], heads, jnp.zeros((5, width), F32)], axis=0
    )
    shared = (gq_rows, gk_rows, gv_rows, grad_logits, w_qkv, wgt, xn1, g1)
    *far, bundle = input_back(cs, 2, *shared, bundle)
    *close, bundle = input_back(cs, 0, *shared, bundle)
    grad_xn1 = scatter_ctx(close + far)
    x = tokens.astype(F32)
    scale1 = lax.rsqrt(jnp.mean(x * x, axis=-1, keepdims=True) + EPS)
    grad_x, _ = norm_back(x, scale1, g1, grad_xn1)
    grad_tokens = grad_hidden1 + grad_x

    g_wo = lax.psum_scatter(grad_wo, "seq", scatter_dimension=0, tiled=True)
    g_wo = turn(g_wo).astype(F32)
    pieces = jnp.concatenate(
        [
            outer(gq_rows, xn1).astype(BF16).reshape(2, 2, 64, width),
            outer(gk_rows, xn1).astype(BF16).reshape(2, 2, 32, width),
            outer(gv_rows, xn1).astype(BF16).reshape(2, 2, 32, width),
        ],
        axis=2,
    )
    for axis, bit in ((1, s & 1), (0, s >> 1)):
        sent = lax.dynamic_index_in_dim(pieces, 1 - bit, axis, keepdims=False)
        kept = lax.dynamic_index_in_dim(pieces, bit, axis, keepdims=False)
        got = hop(sent, 8 if axis else 16)
        pieces = (kept.astype(F32) + got.astype(F32)).astype(BF16)
    home = turn(pieces)
    g_wq, g_wk, g_wv = (v.astype(F32) for v in jnp.split(home, (64, 96), axis=0))

    bundle = sum_small(bundle, pieces)
    blocks = lax.dynamic_slice_in_dim(bundle[:18], 64 * flat, 64, 1)
    heads = lax.dynamic_slice_in_dim(bundle[18, : 2 * HD].reshape(2, HD), 4 * flat, 4, 1)
    return (
        output,
        grad_tokens,
        g_wq,
        g_wk,
        g_wv,
        g_wo,
        blocks[:16],
        blocks[16],
        heads[0],
        heads[1],
        blocks[17],
        grad_w_gate,
        grad_w_up,
        grad_w_down,
    )


def solution(mesh):
    in_specs = (
        P(("seq", "ctx"), None),
        P("seq"),
        P("seq", None),
        P(("seq", "ctx"), None),
        P(("seq", "ctx"), None),
        P(("seq", "ctx"), None),
        P(("seq", "ctx"), None),
        P(None, ("seq", "ctx")),
        P(("seq", "ctx")),
        P(("seq", "ctx")),
        P(("seq", "ctx")),
        P(("seq", "ctx")),
        P(("seq", "ctx"), None),
        P(("seq", "ctx"), None),
        P(("seq", "ctx"), None),
        P(("seq", "ctx"), None),
    )
    out_specs = (
        P(("seq", "ctx"), None),
        P(("seq", "ctx"), None),
        P(("seq", "ctx"), None),
        P(("seq", "ctx"), None),
        P(("seq", "ctx"), None),
        P(("seq", "ctx"), None),
        P(None, ("seq", "ctx")),
        P(("seq", "ctx")),
        P(("seq", "ctx")),
        P(("seq", "ctx")),
        P(("seq", "ctx")),
        P(("seq", "ctx"), None),
        P(("seq", "ctx"), None),
        P(("seq", "ctx"), None),
    )
    sizes = dict(mesh.shape)
    small = sizes == {"seq": 4, "ctx": 8}
    return jax.shard_map(
        per_device_small if small else per_device, mesh=mesh, in_specs=in_specs, out_specs=out_specs, check_vma=False
    )
```
